32 devices in a mesh: seq: 2 (over x), book: 4 (over y, core), head: 4 (over z).
Axes of the slice: x: 2, y: 2, z: 4, core: 2. Of those that a mesh axis runs over, the one named last changes fastest.
Arguments:
- tokens: bfloat16 [4, 1024, 1024], P('book', 'seq'), may hold values from -40 to 40
- w_qkv: bfloat16 [1024, 3, 8, 128], P(None, None, 'head'), may hold values from -0.1875 to 0.1875
- w_out: bfloat16 [8, 128, 1024], P('head'), may hold values from -0.1875 to 0.1875
- slot_queries: bfloat16 [512, 8, 128], P(None, 'head'), may hold values from -40 to 40
- state_proj: bfloat16 [8, 128, 2, 128], P('head'), may hold values from -2.5 to 2.5
- init_state: float32 [4, 512, 8, 128], P('book', None, 'head'), may hold values from -6 to 6
- forget: float32 [4, 2, 8, 128], P('book', 'seq', 'head'), may hold values from 0.02 to 1
Outputs:
- mixed: bfloat16 [4, 1024, 1024], P('book', ('seq', 'head'))
- carried: float32 [4, 2, 512, 8, 128], P('book', 'seq', None, 'head')
The draws below stay inside these ranges and needn't reach their ends.
All inputs are finite; a program needn't handle non-finite values.
Results may differ from the reference program's by a relative error of at most 0.03.
Values may be sent and summed in bfloat16 or wider, within the bound.
A program may use at most 64 MiB of HBM per device.

```python
import math
import jax
import jax.numpy as jnp
from jax import lax

D = 1024
H = 8
HD = 128
S = 512
W = 512
BOOK_BLOCKS = 2
SEQLEN = 1024
BOOK_COUNT = 4


def rough_rows(key, shape):
    component_pieces = jax.random.split(key, 1)
    values = jnp.clip(jax.random.normal(component_pieces[0], shape, jnp.float32), -6.0, 6.0)
    return jnp.clip(values, -40.0, 40.0)


def draw_tokens(key, part):
    return rough_rows(jax.random.fold_in(key, 11), (BOOK_COUNT, SEQLEN, D)).astype(jnp.bfloat16)


def draw_slot_queries(key, part):
    return rough_rows(jax.random.fold_in(key, 23), (S, H, HD)).astype(jnp.bfloat16)


def draw_forget(key, part):
    component_pieces = jax.random.split(jax.random.fold_in(key, 37), 6)
    fast_share = 0.5
    fast = jax.random.uniform(component_pieces[0], (H, HD), jnp.float32) < fast_share
    slow_rate = math.log(10.0) / BOOK_BLOCKS * jax.random.uniform(component_pieces[1], (H, HD), jnp.float32, 0.2, 0.7)
    jitter = jnp.exp(jax.random.uniform(component_pieces[2], (BOOK_COUNT, BOOK_BLOCKS, H, HD), jnp.float32, -0.35, 0.35))
    gradual_retain = jnp.exp(-slow_rate * jitter)
    fast_keep = jax.random.uniform(component_pieces[3], (BOOK_COUNT, BOOK_BLOCKS, H, HD), jnp.float32, 0.02, 0.3)
    sudden_input = jax.random.uniform(component_pieces[4], (BOOK_COUNT, BOOK_BLOCKS, 1, 1), jnp.float32) < 2.0 / BOOK_BLOCKS
    sudden_retain = jax.random.uniform(component_pieces[5], (BOOK_COUNT, BOOK_BLOCKS, 1, 1), jnp.float32, 0.5, 0.8)
    gradual_retain = gradual_retain * jnp.where(sudden_input, sudden_retain, 1.0)
    return jnp.where(fast, fast_keep, gradual_retain).astype(jnp.float32)


def steps_of(own_key, dims, shards, least, largest):
    factor_of = 1.0
    for position, blocks in shards:
        steps = jax.random.uniform(jax.random.fold_in(jax.random.fold_in(own_key, 6), position), (blocks,), jnp.float32, least / len(shards), largest / len(shards))
        factor_of = factor_of * jnp.repeat(jnp.exp(steps), dims[position] // blocks).reshape((-1,) + (1,) * (len(dims) - 1 - position))
    return factor_of


def noise(own_key, extent, scale, most, pieces=(), held_as=jnp.bfloat16):
    drawn = scale * jax.random.normal(own_key, extent, jnp.float32)
    if pieces:
        drawn = drawn * steps_of(own_key, extent, pieces, -0.22, 0.18)
    return jnp.clip(drawn, -most, most).astype(held_as)


def setup_inputs(seed: int = 0) -> dict:
    seeds = jax.random.split(jax.random.key(seed), 8)
    tokens = draw_tokens(jax.random.fold_in(seeds[7], 71), 0)
    w_qkv = noise(seeds[1], (D, 3, H, HD), D ** -0.5, 0.1875, ((2, 4),))
    w_out = noise(seeds[2], (H, HD, D), (H * HD) ** -0.5, 0.1875, ((0, 4),))
    slot_queries = draw_slot_queries(jax.random.fold_in(seeds[7], 71), 0)
    state_proj = noise(seeds[4], (H, HD, 2, HD), (2.0 / HD ** 0.5), 2.5, ((0, 4),))
    init_state = noise(seeds[5], (BOOK_COUNT, S, H, HD), 1.0, 6.0, ((0, 4), (2, 4)), jnp.float32)
    forget = draw_forget(jax.random.fold_in(seeds[7], 71), 0)
    return {"tokens": tokens, "w_qkv": w_qkv, "w_out": w_out, "slot_queries": slot_queries, "state_proj": state_proj, "init_state": init_state, "forget": forget}


def softmax_rows(scores):
    row_max = jnp.max(scores, axis=-1, keepdims=True)
    shifted = jnp.exp(scores - row_max)
    return shifted / jnp.sum(shifted, axis=-1, keepdims=True)


def reference(tokens, w_qkv, w_out, slot_queries, state_proj, init_state, forget):
    score_scale = HD ** -0.5
    slot_float = slot_queries.astype(jnp.float32)
    projection_floating = state_proj.astype(jnp.float32)
    w_flat = w_out.reshape(H * HD, D)

    def one_book(book_args):
        book_rows, book_state, book_forget = book_args
        projected = jnp.dot(book_rows, w_qkv.reshape(D, 3 * H * HD), preferred_element_type=jnp.float32)
        projected = projected.astype(jnp.bfloat16).reshape(BOOK_BLOCKS, W, 3, H, HD)
        block_ids = jnp.arange(BOOK_BLOCKS, dtype=jnp.int32)

        def block_step(carried_in, block_in):
            carry_state, prev_keys, prev_values = carried_in
            block_proj, retain, block_idx = block_in
            query_rows = block_proj[:, 0]
            key_rows = block_proj[:, 1]
            value_rows = block_proj[:, 2]
            slot_scores = jnp.einsum("shd,khd->hsk", slot_float, key_rows.astype(jnp.float32)) * score_scale
            slot_weights = softmax_rows(slot_scores).astype(jnp.bfloat16)
            summary = jnp.einsum("hsk,khd->shd", slot_weights.astype(jnp.float32), value_rows.astype(jnp.float32))
            state_low = carry_state.astype(jnp.bfloat16).astype(jnp.float32)
            state_kv = jnp.einsum("shd,hdce->sche", state_low, projection_floating).astype(jnp.bfloat16)
            key_all = jnp.concatenate([prev_keys, key_rows, state_kv[:, 0]], axis=0)
            value_all = jnp.concatenate([prev_values, value_rows, state_kv[:, 1]], axis=0)
            token_scores = jnp.einsum("qhd,khd->hqk", query_rows.astype(jnp.float32), key_all.astype(jnp.float32)) * score_scale
            row_pos = jnp.arange(W, dtype=jnp.int32)[:, None]
            col_pos = jnp.arange(2 * W + S, dtype=jnp.int32)[None, :]
            local_ok = (col_pos - W <= row_pos) & (col_pos > row_pos) & ((col_pos >= W) | (block_idx > 0))
            allowed = jnp.where(col_pos < 2 * W, local_ok, True)
            token_scores = jnp.where(allowed[None], token_scores, -1e30)
            weights = softmax_rows(token_scores).astype(jnp.bfloat16)
            attended = jnp.einsum("hqk,khd->qhd", weights.astype(jnp.float32), value_all.astype(jnp.float32)).astype(jnp.bfloat16)
            new_state = retain * carry_state + (1.0 - retain) * summary
            return (new_state, key_rows, value_rows), (attended, new_state)

        empty_rows = jnp.zeros((W, H, HD), jnp.bfloat16)
        start_carry = (book_state, empty_rows, empty_rows)
        unused, (attended, carried) = lax.scan(block_step, start_carry, (projected, book_forget, block_ids))
        attended = attended.reshape(SEQLEN, H * HD)
        mixed = jnp.dot(attended, w_flat, preferred_element_type=jnp.float32).astype(jnp.bfloat16)
        return mixed, carried

    mixed, carried = lax.map(one_book, (tokens, init_state, forget))
    return mixed, carried
```

```python
import functools
import jax
import jax.numpy as jnp
from jax import lax
from jax.experimental import pallas as pl
from jax.experimental.pallas import tpu as pltpu
from jax.sharding import PartitionSpec as P

W = 512
MESH = pl.DeviceIdType.MESH
F32 = jnp.float32
BF16 = jnp.bfloat16


def nt_dot(a, b):
    return lax.dot_general(a, b, (((1,), (1,)), ((), ())), preferred_element_type=F32)


def fused_kernel(
    heads, tok_hbm, wqkv_hbm, wout_hbm, sq_hbm, sp_hbm, init_hbm, fg_hbm,
    mixed_hbm, carried_hbm,
    tok, wraw, wf, w2, sqraw, sqf, sqb, spraw, spf, init, fg, fg0,
    kcat, vcat, qb, summ, state, skv, carried, wo, att, att_out, mixed,
    in_sem, out_sem, kv_send, kv_recv, wz_send, wz_recv, wc_send, wc_recv, at_send, at_recv,
):
    seq = lax.axis_index("seq")
    book = lax.axis_index("book")
    head = lax.axis_index("head")
    core = lax.rem(book, 2)
    partner = book + 1 - 2 * core
    hd = kcat.shape[2]
    n_loc = kcat.shape[0]
    slots = sqb.shape[1]
    depth = tok.shape[1]
    rows = att.shape[1]
    half = wo.shape[1] // 2
    scale = hd ** (-0.5)

    loads = [
        pltpu.make_async_copy(src, dst, in_sem.at[i])
        for i, (src, dst) in enumerate(
            [(wqkv_hbm, wraw), (tok_hbm, tok), (sq_hbm, sqraw), (init_hbm, init),
             (fg_hbm, fg), (sp_hbm, spraw), (wout_hbm, wo.at[head])]
        )
    ]
    for load in loads:
        load.start()

    barrier = pltpu.get_barrier_semaphore()
    peers = [lax.rem(head + step, heads) for step in range(1, heads)]
    for peer in peers:
        pl.semaphore_signal(barrier, inc=1, device_id={"head": peer}, device_id_type=MESH)
    pl.semaphore_signal(barrier, inc=1, device_id={"book": partner}, device_id_type=MESH)
    pl.semaphore_signal(barrier, inc=1, device_id={"seq": 1 - seq}, device_id_type=MESH)
    pl.semaphore_wait(barrier, heads + 1)

    mine = pl.ds(pl.multiple_of(core * half, half), half)
    wz = [
        pltpu.make_async_remote_copy(
            src_ref=wout_hbm.at[mine], dst_ref=wo.at[head, mine],
            send_sem=wz_send.at[step], recv_sem=wz_recv.at[step],
            device_id={"head": peer}, device_id_type=MESH,
        )
        for step, peer in enumerate(peers)
    ]
    wc = []
    for step in range(heads - 1):
        origin = lax.rem(head + heads - (step + 1), heads)
        wc.append(
            pltpu.make_async_remote_copy(
                src_ref=wo.at[origin, mine], dst_ref=wo.at[origin, mine],
                send_sem=wc_send.at[step], recv_sem=wc_recv.at[step],
                device_id={"book": partner}, device_id_type=MESH,
            )
        )

    def kv_copy(idx, src, dst):
        return pltpu.make_async_remote_copy(
            src_ref=src, dst_ref=dst, send_sem=kv_send.at[idx], recv_sem=kv_recv.at[idx],
            device_id={"seq": 1 - seq}, device_id_type=MESH,
        )

    kv = [kv_copy(0, fg_hbm, fg0)]
    for h in range(n_loc):
        kv.append(kv_copy(1 + 2 * h, kcat.at[h, pl.ds(W, W)], kcat.at[h, pl.ds(0, W)]))
        kv.append(kv_copy(2 + 2 * h, vcat.at[h, pl.ds(W, W)], vcat.at[h, pl.ds(0, W)]))

    @pl.when(seq == 0)
    def _():
        kv[0].start()

    for copy in wz:
        copy.start()

    loads[0].wait()
    wf[...] = wraw[...].astype(F32)
    period = 3 * n_loc

    def project(part):
        for h in range(n_loc):
            w2[part, :, h * hd:(h + 1) * hd] = wf[
                pl.ds(part * n_loc + h, depth, stride=period), :
            ].astype(BF16)
        return jnp.dot(tok[...], w2[part], preferred_element_type=F32).astype(BF16)

    loads[1].wait()
    keys = project(1)
    for h in range(n_loc):
        kcat[h, W:, :] = keys[:, h * hd:(h + 1) * hd]

    @pl.when(seq == 0)
    def _():
        kv[1].start()

    values = project(2)
    for h in range(n_loc):
        vcat[h, W:, :] = values[:, h * hd:(h + 1) * hd]

    @pl.when(seq == 0)
    def _():
        for copy in kv[2:]:
            copy.start()

    queries = project(0)
    for h in range(n_loc):
        qb[h] = queries[:, h * hd:(h + 1) * hd]

    loads[2].wait()
    sqf[...] = sqraw[...].astype(F32)
    for h in range(n_loc):
        sqb[h] = sqf[pl.ds(h, slots, stride=n_loc), :].astype(BF16)
    loads[5].wait()
    spf[...] = spraw[...].astype(F32)
    loads[3].wait()
    loads[4].wait()

    tile = 256

    def slot_summary(h, row, off):
        scores = nt_dot(sqb[h, row:row + tile, :], kcat[h, off:off + W, :])
        top = jnp.max(scores, axis=1, keepdims=True)
        p = jnp.exp((scores - top) * scale)
        total = jnp.sum(p, axis=1, keepdims=True)
        part = jnp.dot(p.astype(BF16), vcat[h, off:off + W, :], preferred_element_type=F32)
        return part / total

    for h in range(n_loc):
        for row in range(0, slots, tile):
            summ[h, row:row + tile, :] = slot_summary(h, row, W)

    @pl.when(seq == 0)
    def _():
        for h in range(n_loc):
            kcat[h, :W, :] = jnp.zeros((W, hd), BF16)
            vcat[h, :W, :] = jnp.zeros((W, hd), BF16)
            state[h] = init[pl.ds(h, slots, stride=n_loc), :]

    @pl.when(seq == 1)
    def _():
        kv[0].wait_recv()
        for h in range(n_loc):
            kv[1 + 2 * h].wait_recv()
            kv[2 + 2 * h].wait_recv()
            keep = fg0[h:h + 1, :]
            for row in range(0, slots, tile):
                first = init[pl.ds(h + n_loc * row, tile, stride=n_loc), :]
                state[h, row:row + tile, :] = keep * first + (1.0 - keep) * slot_summary(h, row, 0)

    for h in range(n_loc):
        keep = fg[h:h + 1, :]
        base = h * 2 * hd
        proj = jnp.concatenate(
            [spf[pl.ds(base + c, hd, stride=2), :].astype(BF16) for c in range(2)], axis=1
        )
        skv[h] = jnp.dot(state[h].astype(BF16), proj, preferred_element_type=F32).astype(BF16)
        carried[pl.ds(h, slots, stride=n_loc), :] = keep * state[h] + (1.0 - keep) * summ[h]
    carried_out = pltpu.make_async_copy(carried, carried_hbm, out_sem.at[0])
    carried_out.start()

    span = W + rows
    r_pos = lax.broadcasted_iota(jnp.int32, (rows, span), 0)
    c_pos = lax.broadcasted_iota(jnp.int32, (rows, span), 1)
    window = (c_pos > r_pos) & (c_pos <= r_pos + W)
    floor = W * (1 - seq)

    def attend(start, h):
        q = qb[h, pl.ds(start, rows), :]
        near = nt_dot(q, kcat[h, pl.ds(start, span), :])
        allowed = window & (c_pos + start >= floor)
        near = jnp.where(allowed, near, -1e30)
        far = nt_dot(q, skv[h, :, :hd])
        top = jnp.maximum(
            jnp.max(near, axis=1, keepdims=True), jnp.max(far, axis=1, keepdims=True)
        )
        p_near = jnp.exp((near - top) * scale)
        p_far = jnp.exp((far - top) * scale)
        total = jnp.sum(p_near, axis=1, keepdims=True) + jnp.sum(p_far, axis=1, keepdims=True)
        out = jnp.dot(
            p_near.astype(BF16), vcat[h, pl.ds(start, span), :], preferred_element_type=F32
        ) + jnp.dot(p_far.astype(BF16), skv[h, :, hd:], preferred_element_type=F32)
        return (out / total).astype(BF16)

    sends = []
    for step in range(heads):
        goal = lax.rem(head + step + 1, heads)
        start = pl.multiple_of(goal * rows, rows)
        for h in range(n_loc):
            if step < heads - 1:
                att_out[step, :, h * hd:(h + 1) * hd] = attend(start, h)
            else:
                att[head, :, h * hd:(h + 1) * hd] = attend(start, h)
        if step < heads - 1:
            copy = pltpu.make_async_remote_copy(
                src_ref=att_out.at[step], dst_ref=att.at[head],
                send_sem=at_send.at[step], recv_sem=at_recv.at[step],
                device_id={"head": goal}, device_id_type=MESH,
            )
            copy.start()
            sends.append(copy)

    for step in range(heads - 1):
        wz[step].wait_recv()
        wc[step].start()

    loads[6].wait()
    acc = jnp.dot(att[head], wo[head], preferred_element_type=F32)
    for step in range(heads - 1):
        origin = lax.rem(head + heads - (step + 1), heads)
        wc[step].wait_recv()
        sends[step].wait_recv()
        acc = acc + jnp.dot(att[origin], wo[origin], preferred_element_type=F32)
    mixed[...] = acc.astype(BF16)
    mixed_out = pltpu.make_async_copy(mixed, mixed_hbm, out_sem.at[1])
    mixed_out.start()

    for step in range(heads - 1):
        wz[step].wait_send()
        wc[step].wait_send()
        sends[step].wait_send()

    @pl.when(seq == 0)
    def _():
        for copy in kv:
            copy.wait_send()

    carried_out.wait()
    mixed_out.wait()


def fused_local(heads, tokens, w_qkv, w_out, slot_queries, state_proj, init_state, forget):
    tok_dev, depth = tokens.shape[1:]
    n_loc, hd = w_qkv.shape[2:]
    slots = slot_queries.shape[0]
    rows = tok_dev // heads
    period = 3 * n_loc
    anywhere = pl.BlockSpec(memory_space=pl.ANY)
    v = pltpu.VMEM
    dma = pltpu.SemaphoreType.DMA
    mixed, carried = pl.pallas_call(
        functools.partial(fused_kernel, heads),
        out_shape=(
            jax.ShapeDtypeStruct((rows, depth), BF16),
            jax.ShapeDtypeStruct((slots * n_loc, hd), F32),
        ),
        in_specs=[anywhere] * 7,
        out_specs=(anywhere, anywhere),
        scratch_shapes=[
            v((tok_dev, depth), BF16),
            v((depth * period, hd), BF16),
            v((depth * period, hd), F32),
            v((3, depth, n_loc * hd), BF16),
            v((slots * n_loc, hd), BF16),
            v((slots * n_loc, hd), F32),
            v((n_loc, slots, hd), BF16),
            v((n_loc * hd * 2, hd), BF16),
            v((n_loc * hd * 2, hd), F32),
            v((slots * n_loc, hd), F32),
            v((n_loc, hd), F32),
            v((n_loc, hd), F32),
            v((n_loc, 2 * W, hd), BF16),
            v((n_loc, 2 * W, hd), BF16),
            v((n_loc, tok_dev, hd), BF16),
            v((n_loc, slots, hd), F32),
            v((n_loc, slots, hd), F32),
            v((n_loc, slots, 2 * hd), BF16),
            v((slots * n_loc, hd), F32),
            v((heads, n_loc * hd, depth), BF16),
            v((heads, rows, n_loc * hd), BF16),
            v((heads - 1, rows, n_loc * hd), BF16),
            v((rows, depth), BF16),
            dma((7,)),
            dma((2,)),
            dma((1 + 2 * n_loc,)),
            dma((1 + 2 * n_loc,)),
            dma((heads - 1,)),
            dma((heads - 1,)),
            dma((heads - 1,)),
            dma((heads - 1,)),
            dma((heads - 1,)),
            dma((heads - 1,)),
        ],
        compiler_params=pltpu.CompilerParams(
            collective_id=0, has_side_effects=True, vmem_limit_bytes=48 * 1024 * 1024
        ),
        name="fused_layer",
    )(
        tokens[0],
        w_qkv.reshape(depth * period, hd),
        w_out.reshape(n_loc * hd, depth),
        slot_queries.reshape(slots * n_loc, hd),
        state_proj.reshape(n_loc * hd * 2, hd),
        init_state.reshape(slots * n_loc, hd),
        forget.reshape(n_loc, hd),
    )
    return mixed.reshape(1, rows, depth), carried.reshape(1, 1, slots, n_loc, hd)


def from_behind(block, axis, distance):
    devices = range(lax.axis_size(axis))
    route = [(i - distance, i) for i in devices if i - distance in devices]
    return lax.ppermute(block, axis, route)


def softmax_rows(scores):
    row_max = jnp.max(scores, axis=-1, keepdims=True)
    shifted = jnp.exp(scores - row_max)
    return shifted / jnp.sum(shifted, axis=-1, keepdims=True)


def local(tokens, w_qkv, w_out, slot_queries, state_proj, init_state, forget):
    tok_dev = tokens.shape[1]
    model_width = tokens.shape[2]
    head_count = w_qkv.shape[2]
    head_dim = w_qkv.shape[3]
    blocks_dev = tok_dev // W
    score_scale = head_dim ** (-0.5)
    projected = jnp.dot(
        tokens[0],
        w_qkv.reshape(model_width, 3 * head_count * head_dim),
        preferred_element_type=jnp.float32,
    )
    projected = projected.astype(jnp.bfloat16).reshape(tok_dev, 3, head_count, head_dim)
    query_rows = projected[:, 0]
    key_rows = projected[:, 1]
    value_rows = projected[:, 2]
    last_rows = jnp.stack([key_rows, value_rows], axis=0)
    before = from_behind(last_rows, "seq", 1)
    position = lax.axis_index("seq")
    retain = forget[0]
    slot_scores = (
        jnp.einsum("shd,khd->hsk", slot_queries, key_rows, preferred_element_type=jnp.float32)
        * score_scale
    )
    slot_weights = softmax_rows(slot_scores).astype(jnp.bfloat16)
    summaries = [
        jnp.einsum("hsk,khd->shd", slot_weights, value_rows, preferred_element_type=jnp.float32)
    ]
    decay_all = jnp.ones((head_count, head_dim), jnp.float32)
    offset = jnp.zeros(summaries[0].shape, jnp.float32)
    block_idx = 0
    decay_all = decay_all * retain[block_idx]
    offset = retain[block_idx] * offset + (1.0 - retain[block_idx]) * summaries[block_idx]
    initial = init_state[0]

    def relay_step(round_idx, current):
        passed = from_behind(decay_all * current + offset, "seq", 1)
        return jnp.where(position == 0, initial, passed)

    arriving_state = lax.fori_loop(0, lax.axis_size("seq") - 1, relay_step, initial)
    carry_state = arriving_state
    row_pos = jnp.arange(W, dtype=jnp.int32)[:, None]
    col_pos = jnp.arange(2 * W + slot_queries.shape[0], dtype=jnp.int32)[None, :]
    block_idx = 0
    prev_keys = before[0]
    prev_values = before[1]
    state_kv = jnp.einsum(
        "shd,hdce->sche",
        carry_state.astype(jnp.bfloat16),
        state_proj,
        preferred_element_type=jnp.float32,
    ).astype(jnp.bfloat16)
    key_all = jnp.concatenate([prev_keys, key_rows, state_kv[:, 0]], axis=0)
    value_all = jnp.concatenate([prev_values, value_rows, state_kv[:, 1]], axis=0)
    token_scores = (
        jnp.einsum("qhd,khd->hqk", query_rows, key_all, preferred_element_type=jnp.float32)
        * score_scale
    )
    global_block = position * blocks_dev + block_idx
    local_ok = (
        (col_pos - W <= row_pos) & (col_pos > row_pos) & ((col_pos >= W) | (global_block > 0))
    )
    allowed = jnp.where(col_pos < 2 * W, local_ok, True)
    token_scores = jnp.where(allowed[None], token_scores, -1e30)
    weights = softmax_rows(token_scores).astype(jnp.bfloat16)
    attended_blocks = jnp.einsum(
        "hqk,khd->qhd", weights, value_all, preferred_element_type=jnp.float32
    ).astype(jnp.bfloat16)
    carry_state = retain[block_idx] * carry_state + (1.0 - retain[block_idx]) * summaries[block_idx]
    carried_blocks = [carry_state]
    attended = attended_blocks.reshape(tok_dev, head_count * head_dim)
    w_flat = w_out.reshape(head_count * head_dim, model_width)
    row_share = tok_dev // lax.axis_size("head")
    partial_out = jnp.dot(attended, w_flat, preferred_element_type=jnp.float32)
    mixed_rows = lax.psum_scatter(partial_out, "head", scatter_dimension=0, tiled=True)
    mixed = mixed_rows.astype(jnp.bfloat16).reshape(1, row_share, model_width)
    carried = jnp.stack(carried_blocks, axis=0)[None]
    return (mixed, carried)


def solution(mesh):
    placed = (
        P("book", "seq", None),
        P(None, None, "head", None),
        P("head", None, None),
        P(None, "head", None),
        P("head", None, None, None),
        P("book", None, "head", None),
        P("book", "seq", "head", None),
    )
    body = functools.partial(fused_local, mesh.shape["head"]) if mesh.shape["seq"] == 2 else local
    return jax.shard_map(
        body,
        mesh=mesh,
        in_specs=placed,
        out_specs=(P("book", ("seq", "head"), None), P("book", "seq", None, "head", None)),
        check_vma=False,
    )
```

```python
import functools
import jax
import jax.numpy as jnp
from jax import lax
from jax.experimental import pallas as pl
from jax.experimental.pallas import tpu as pltpu
from jax.sharding import PartitionSpec as P

W = 512
MESH = pl.DeviceIdType.MESH
F32 = jnp.float32
BF16 = jnp.bfloat16


def nt_dot(a, b):
    return lax.dot_general(a, b, (((1,), (1,)), ((), ())), preferred_element_type=F32)


def fused_kernel(
    heads, tok_hbm, wqkv_hbm, wout_hbm, sq_hbm, sp_hbm, init_hbm, fg_hbm,
    mixed_hbm, carried_hbm,
    tok, wraw, wf, w2, sqraw, sqf, sqb, spraw, spf, init, fg, fg0,
    kcat, vcat, qb, summ, state, skv, own_acc, own_max, own_sum, carried, wo, att, att_out, mixed,
    in_sem, out_sem, kv_send, kv_recv, wz_send, wz_recv, wy_send, wy_recv,
    wc_send, wc_recv, wd_send, wd_recv, at_send, at_recv,
):
    seq = lax.axis_index("seq")
    book = lax.axis_index("book")
    head = lax.axis_index("head")
    core = lax.rem(book, 2)
    side = book // 2
    core_mate = book + 1 - 2 * core
    side_mate = lax.rem(book + 2, 4)
    hd = kcat.shape[2]
    n_loc = kcat.shape[0]
    slots = sqb.shape[1]
    depth = tok.shape[1]
    rows = att.shape[2]
    part_rows = hd // 2
    scale = hd ** (-0.5)

    loads = [
        pltpu.make_async_copy(src, dst, in_sem.at[i])
        for i, (src, dst) in enumerate(
            [(wqkv_hbm, wraw), (tok_hbm, tok), (sq_hbm, sqraw), (init_hbm, init),
             (fg_hbm, fg), (sp_hbm, spraw), (wout_hbm, wo.at[:, head])]
        )
    ]
    for load in loads:
        load.start()

    barrier = pltpu.get_barrier_semaphore()
    peers = [lax.rem(head + step, heads) for step in range(1, heads)]
    origins = [lax.rem(head + heads - step, heads) for step in range(1, heads)]
    for peer in peers:
        pl.semaphore_signal(barrier, inc=1, device_id={"head": peer}, device_id_type=MESH)
    pl.semaphore_signal(barrier, inc=1, device_id={"book": core_mate}, device_id_type=MESH)
    pl.semaphore_signal(barrier, inc=1, device_id={"book": side_mate}, device_id_type=MESH)
    pl.semaphore_signal(barrier, inc=1, device_id={"seq": 1 - seq}, device_id_type=MESH)

    mine = pl.ds(pl.multiple_of(core * part_rows, part_rows), part_rows)

    def remote(src, dst, send, recv, goal):
        return pltpu.make_async_remote_copy(
            src_ref=src, dst_ref=dst, send_sem=send, recv_sem=recv,
            device_id=goal, device_id_type=MESH,
        )

    steps = range(heads - 1)
    wz = [
        remote(wout_hbm.at[side, mine], wo.at[side, head, mine], wz_send.at[i], wz_recv.at[i],
               {"head": peers[i]})
        for i in steps
    ]
    near = [wo.at[side, origins[i], mine] for i in steps]
    across = [wo.at[1 - side, origins[i], mine] for i in steps]
    wy = [remote(near[i], near[i], wy_send.at[i], wy_recv.at[i], {"book": side_mate}) for i in steps]
    wc = [remote(near[i], near[i], wc_send.at[i], wc_recv.at[i], {"book": core_mate}) for i in steps]
    wd = [
        remote(across[i], across[i], wd_send.at[i], wd_recv.at[i], {"book": core_mate})
        for i in steps
    ]

    def kv_copy(idx, src, dst):
        return remote(src, dst, kv_send.at[idx], kv_recv.at[idx], {"seq": 1 - seq})

    kv = [kv_copy(0, fg_hbm, fg0)]
    for h in range(n_loc):
        kv.append(kv_copy(1 + 2 * h, kcat.at[h, pl.ds(W, W)], kcat.at[h, pl.ds(0, W)]))
        kv.append(kv_copy(2 + 2 * h, vcat.at[h, pl.ds(W, W)], vcat.at[h, pl.ds(0, W)]))

    loads[0].wait()
    wf[...] = wraw[...].astype(F32)
    period = 3 * n_loc

    def project(slot, columns):
        for i, column in enumerate(columns):
            w2[slot, :, i * hd:(i + 1) * hd] = wf[pl.ds(column, depth, stride=period), :].astype(BF16)
        return jnp.dot(tok[...], w2[slot], preferred_element_type=F32).astype(BF16)

    loads[1].wait()
    for h in range(n_loc):
        both = project(h, (n_loc + h, 2 * n_loc + h))
        kcat[h, W:, :] = both[:, :hd]
        vcat[h, W:, :] = both[:, hd:]
        if h == 0:
            pl.semaphore_wait(barrier, heads + 2)

        @pl.when(seq == 0)
        def _():
            kv[1 + 2 * h].start()
            kv[2 + 2 * h].start()
            if h == 0:
                kv[0].start()

        if h == 0:
            for copy in wz:
                copy.start()

    queries = project(n_loc, range(n_loc))
    for h in range(n_loc):
        qb[h] = queries[:, h * hd:(h + 1) * hd]

    loads[2].wait()
    sqf[...] = sqraw[...].astype(F32)
    for h in range(n_loc):
        sqb[h] = sqf[pl.ds(h, slots, stride=n_loc), :].astype(BF16)
    loads[5].wait()
    spf[...] = spraw[...].astype(F32)
    loads[3].wait()
    loads[4].wait()

    tile = 256

    def slot_summary(h, row, off):
        scores = nt_dot(sqb[h, row:row + tile, :], kcat[h, off:off + W, :])
        top = jnp.max(scores, axis=1, keepdims=True)
        p = jnp.exp((scores - top) * scale)
        total = jnp.sum(p, axis=1, keepdims=True)
        part = jnp.dot(p.astype(BF16), vcat[h, off:off + W, :], preferred_element_type=F32)
        return part / total

    for h in range(n_loc):
        for row in range(0, slots, tile):
            summ[h, row:row + tile, :] = slot_summary(h, row, W)

    r_pos = lax.broadcasted_iota(jnp.int32, (rows, rows), 0)
    c_pos = lax.broadcasted_iota(jnp.int32, (rows, rows), 1)
    causal = c_pos <= r_pos

    def masked(scores, at, allowed):
        blocks = [scores[:, c:c + rows] for c in range(0, scores.shape[1], rows)]
        blocks[at] = jnp.where(allowed, blocks[at], -1e30)
        return jnp.concatenate(blocks, axis=1)

    for h in range(n_loc):
        for i in range(heads):
            q = qb[h, i * rows:(i + 1) * rows, :]
            stop = W + (i + 1) * rows
            scores = masked(nt_dot(q, kcat[h, W:stop, :]), i, causal)
            top = jnp.max(scores, axis=1, keepdims=True)
            p = jnp.exp((scores - top) * scale)
            own_max[h, i] = top
            own_sum[h, i] = jnp.sum(p, axis=1, keepdims=True)
            own_acc[h, i] = jnp.dot(p.astype(BF16), vcat[h, W:stop, :], preferred_element_type=F32)

    for i in steps:
        wz[i].wait_recv()
        wy[i].start()
        wc[i].start()

    def attend(h, i, with_prev):
        q = qb[h, i * rows:(i + 1) * rows, :]
        begin = i * rows
        far = nt_dot(q, skv[h, :, :hd])
        top = jnp.maximum(own_max[h, i], jnp.max(far, axis=1, keepdims=True))
        if with_prev:
            prev = masked(nt_dot(q, kcat[h, begin:W, :]), 0, jnp.logical_not(causal))
            top = jnp.maximum(top, jnp.max(prev, axis=1, keepdims=True))
        fade = jnp.exp((own_max[h, i] - top) * scale)
        p_far = jnp.exp((far - top) * scale)
        total = own_sum[h, i] * fade + jnp.sum(p_far, axis=1, keepdims=True)
        out = own_acc[h, i] * fade + jnp.dot(
            p_far.astype(BF16), skv[h, :, hd:], preferred_element_type=F32
        )
        if with_prev:
            p_prev = jnp.exp((prev - top) * scale)
            total = total + jnp.sum(p_prev, axis=1, keepdims=True)
            out = out + jnp.dot(
                p_prev.astype(BF16), vcat[h, begin:W, :], preferred_element_type=F32
            )
        att_out[h, i] = (out / total).astype(BF16)

    def at_copy(h, step):
        goal = lax.rem(head + step + 1, heads)
        return remote(att_out.at[h, goal], att.at[h, head], at_send.at[h, step],
                      at_recv.at[h, step], {"head": goal})

    for h in range(n_loc):
        @pl.when(seq == 0)
        def _():
            state[h] = init[pl.ds(h, slots, stride=n_loc), :]

        @pl.when(seq == 1)
        def _():
            if h == 0:
                kv[0].wait_recv()
            kv[1 + 2 * h].wait_recv()
            kv[2 + 2 * h].wait_recv()
            keep = fg0[h:h + 1, :]
            for row in range(0, slots, tile):
                first = init[pl.ds(h + n_loc * row, tile, stride=n_loc), :]
                state[h, row:row + tile, :] = keep * first + (1.0 - keep) * slot_summary(h, row, 0)

        base = h * 2 * hd
        proj = jnp.concatenate(
            [spf[pl.ds(base + c, hd, stride=2), :].astype(BF16) for c in range(2)], axis=1
        )
        skv[h] = jnp.dot(state[h].astype(BF16), proj, preferred_element_type=F32).astype(BF16)

        @pl.loop(0, heads)
        def _(step):
            goal = lax.rem(head + step + 1, heads)
            for i in range(heads):
                for s in range(2):
                    @pl.when((goal == i) & (seq == s))
                    def _():
                        attend(h, i, s == 1)

            @pl.when(step < heads - 1)
            def _():
                at_copy(h, step).start()

        keep = fg[h:h + 1, :]
        carried[pl.ds(h, slots, stride=n_loc), :] = keep * state[h] + (1.0 - keep) * summ[h]
        if h == 0:
            for i in steps:
                wy[i].wait_recv()
                wd[i].start()

    carried_out = pltpu.make_async_copy(carried, carried_hbm, out_sem.at[0])
    carried_out.start()

    loads[6].wait()
    for i in steps:
        wc[i].wait_recv()
        wd[i].wait_recv()
    for h in range(n_loc):
        att[h, head] = att_out[h, head]
        for step in steps:
            at_copy(h, step).wait_recv()
        gathered = jnp.concatenate([att[h, o] for o in range(heads)], axis=1)
        share = jnp.dot(gathered, wo[h].reshape(heads * hd, depth), preferred_element_type=F32)
        acc = share if h == 0 else acc + share
    mixed[...] = acc.astype(BF16)
    mixed_out = pltpu.make_async_copy(mixed, mixed_hbm, out_sem.at[1])
    mixed_out.start()

    for i in steps:
        for copy in (wz[i], wy[i], wc[i], wd[i]):
            copy.wait_send()
        for h in range(n_loc):
            at_copy(h, i).wait_send()

    @pl.when(seq == 0)
    def _():
        for copy in kv:
            copy.wait_send()

    carried_out.wait()
    mixed_out.wait()


def fused_local(heads, tokens, w_qkv, w_out, slot_queries, state_proj, init_state, forget):
    tok_dev, depth = tokens.shape[1:]
    n_loc, hd = w_qkv.shape[2:]
    slots = slot_queries.shape[0]
    rows = tok_dev // heads
    period = 3 * n_loc
    anywhere = pl.BlockSpec(memory_space=pltpu.HBM)
    v = pltpu.VMEM
    dma = pltpu.SemaphoreType.DMA
    mixed, carried = pl.pallas_call(
        functools.partial(fused_kernel, heads),
        out_shape=(
            jax.ShapeDtypeStruct((rows, depth), BF16),
            jax.ShapeDtypeStruct((slots * n_loc, hd), F32),
        ),
        in_specs=[anywhere] * 7,
        out_specs=(anywhere, anywhere),
        scratch_shapes=[
            v((tok_dev, depth), BF16),
            v((depth * period, hd), BF16),
            v((depth * period, hd), F32),
            v((3, depth, n_loc * hd), BF16),
            v((slots * n_loc, hd), BF16),
            v((slots * n_loc, hd), F32),
            v((n_loc, slots, hd), BF16),
            v((n_loc * hd * 2, hd), BF16),
            v((n_loc * hd * 2, hd), F32),
            v((slots * n_loc, hd), F32),
            v((n_loc, hd), F32),
            v((n_loc, hd), F32),
            v((n_loc, 2 * W, hd), BF16),
            v((n_loc, 2 * W, hd), BF16),
            v((n_loc, tok_dev, hd), BF16),
            v((n_loc, slots, hd), F32),
            v((n_loc, slots, hd), F32),
            v((n_loc, slots, 2 * hd), BF16),
            v((n_loc, heads, rows, hd), F32),
            v((n_loc, heads, rows, 1), F32),
            v((n_loc, heads, rows, 1), F32),
            v((slots * n_loc, hd), F32),
            v((n_loc, heads, hd, depth), BF16),
            v((n_loc, heads, rows, hd), BF16),
            v((n_loc, heads, rows, hd), BF16),
            v((rows, depth), BF16),
            dma((7,)),
            dma((2,)),
            dma((1 + 2 * n_loc,)),
            dma((1 + 2 * n_loc,)),
            *[dma((heads - 1,)) for _ in range(8)],
            dma((n_loc, heads - 1)),
            dma((n_loc, heads - 1)),
        ],
        compiler_params=pltpu.CompilerParams(
            collective_id=0, has_side_effects=True, vmem_limit_bytes=63 * 1024 * 1024
        ),
        name="fused_layer",
    )(
        tokens[0],
        w_qkv.reshape(depth * period, hd),
        w_out,
        slot_queries.reshape(slots * n_loc, hd),
        state_proj.reshape(n_loc * hd * 2, hd),
        init_state.reshape(slots * n_loc, hd),
        forget.reshape(n_loc, hd),
    )
    return mixed.reshape(1, rows, depth), carried.reshape(1, 1, slots, n_loc, hd)


def from_behind(block, axis, distance):
    devices = range(lax.axis_size(axis))
    route = [(i - distance, i) for i in devices if i - distance in devices]
    return lax.ppermute(block, axis, route)


def softmax_rows(scores):
    row_max = jnp.max(scores, axis=-1, keepdims=True)
    shifted = jnp.exp(scores - row_max)
    return shifted / jnp.sum(shifted, axis=-1, keepdims=True)


def local(tokens, w_qkv, w_out, slot_queries, state_proj, init_state, forget):
    tok_dev = tokens.shape[1]
    model_width = tokens.shape[2]
    head_count = w_qkv.shape[2]
    head_dim = w_qkv.shape[3]
    blocks_dev = tok_dev // W
    score_scale = head_dim ** (-0.5)
    projected = jnp.dot(
        tokens[0],
        w_qkv.reshape(model_width, 3 * head_count * head_dim),
        preferred_element_type=jnp.float32,
    )
    projected = projected.astype(jnp.bfloat16).reshape(tok_dev, 3, head_count, head_dim)
    query_rows = projected[:, 0]
    key_rows = projected[:, 1]
    value_rows = projected[:, 2]
    last_rows = jnp.stack([key_rows, value_rows], axis=0)
    before = from_behind(last_rows, "seq", 1)
    position = lax.axis_index("seq")
    retain = forget[0]
    slot_scores = (
        jnp.einsum("shd,khd->hsk", slot_queries, key_rows, preferred_element_type=jnp.float32)
        * score_scale
    )
    slot_weights = softmax_rows(slot_scores).astype(jnp.bfloat16)
    summaries = [
        jnp.einsum("hsk,khd->shd", slot_weights, value_rows, preferred_element_type=jnp.float32)
    ]
    decay_all = jnp.ones((head_count, head_dim), jnp.float32)
    offset = jnp.zeros(summaries[0].shape, jnp.float32)
    block_idx = 0
    decay_all = decay_all * retain[block_idx]
    offset = retain[block_idx] * offset + (1.0 - retain[block_idx]) * summaries[block_idx]
    initial = init_state[0]

    def relay_step(round_idx, current):
        passed = from_behind(decay_all * current + offset, "seq", 1)
        return jnp.where(position == 0, initial, passed)

    arriving_state = lax.fori_loop(0, lax.axis_size("seq") - 1, relay_step, initial)
    carry_state = arriving_state
    row_pos = jnp.arange(W, dtype=jnp.int32)[:, None]
    col_pos = jnp.arange(2 * W + slot_queries.shape[0], dtype=jnp.int32)[None, :]
    block_idx = 0
    prev_keys = before[0]
    prev_values = before[1]
    state_kv = jnp.einsum(
        "shd,hdce->sche",
        carry_state.astype(jnp.bfloat16),
        state_proj,
        preferred_element_type=jnp.float32,
    ).astype(jnp.bfloat16)
    key_all = jnp.concatenate([prev_keys, key_rows, state_kv[:, 0]], axis=0)
    value_all = jnp.concatenate([prev_values, value_rows, state_kv[:, 1]], axis=0)
    token_scores = (
        jnp.einsum("qhd,khd->hqk", query_rows, key_all, preferred_element_type=jnp.float32)
        * score_scale
    )
    global_block = position * blocks_dev + block_idx
    local_ok = (
        (col_pos - W <= row_pos) & (col_pos > row_pos) & ((col_pos >= W) | (global_block > 0))
    )
    allowed = jnp.where(col_pos < 2 * W, local_ok, True)
    token_scores = jnp.where(allowed[None], token_scores, -1e30)
    weights = softmax_rows(token_scores).astype(jnp.bfloat16)
    attended_blocks = jnp.einsum(
        "hqk,khd->qhd", weights, value_all, preferred_element_type=jnp.float32
    ).astype(jnp.bfloat16)
    carry_state = retain[block_idx] * carry_state + (1.0 - retain[block_idx]) * summaries[block_idx]
    carried_blocks = [carry_state]
    attended = attended_blocks.reshape(tok_dev, head_count * head_dim)
    w_flat = w_out.reshape(head_count * head_dim, model_width)
    row_share = tok_dev // lax.axis_size("head")
    partial_out = jnp.dot(attended, w_flat, preferred_element_type=jnp.float32)
    mixed_rows = lax.psum_scatter(partial_out, "head", scatter_dimension=0, tiled=True)
    mixed = mixed_rows.astype(jnp.bfloat16).reshape(1, row_share, model_width)
    carried = jnp.stack(carried_blocks, axis=0)[None]
    return (mixed, carried)


def solution(mesh):
    placed = (
        P("book", "seq", None),
        P(None, None, "head", None),
        P("head", None, None),
        P(None, "head", None),
        P("head", None, None, None),
        P("book", None, "head", None),
        P("book", "seq", "head", None),
    )
    sizes = (mesh.shape["seq"], mesh.shape["book"], mesh.shape["head"])
    body = functools.partial(fused_local, 4) if sizes == (2, 4, 4) else local
    return jax.shard_map(
        body,
        mesh=mesh,
        in_specs=placed,
        out_specs=(P("book", ("seq", "head"), None), P("book", "seq", None, "head", None)),
        check_vma=False,
    )
```

```python
import functools
import jax
import jax.numpy as jnp
from jax import lax
from jax.experimental import pallas as pl
from jax.experimental.pallas import tpu as pltpu
from jax.sharding import PartitionSpec as P

W = 512
MESH = pl.DeviceIdType.MESH
F32 = jnp.float32
BF16 = jnp.bfloat16


def nt_dot(a, b):
    return lax.dot_general(a, b, (((1,), (1,)), ((), ())), preferred_element_type=F32)


def fused_kernel(
    heads, tok_hbm, wqkv_hbm, wout_hbm, sq_hbm, sp_hbm, init_hbm, fg_hbm,
    mixed_hbm, carried_hbm,
    tok, wraw, wf, w2, sqraw, sqf, sqb, spraw, spf, init, fg, fg0,
    kcat, vcat, qb, summ, state, skv, own_acc, own_max, own_sum, carried, wo, att, att_out, mixed,
    in_sem, w_sem, out_sem, kv_send, kv_recv, wz_send, wz_recv, wy_send, wy_recv,
    wc_send, wc_recv, wd_send, wd_recv, at_send, at_recv,
):
    seq = lax.axis_index("seq")
    book = lax.axis_index("book")
    head = lax.axis_index("head")
    core = lax.rem(book, 2)
    side = book // 2
    core_mate = book + 1 - 2 * core
    side_mate = lax.rem(book + 2, 4)
    hd = kcat.shape[2]
    n_loc = kcat.shape[0]
    slots = sqb.shape[1]
    depth = tok.shape[1]
    rows = att.shape[2]
    part_rows = hd // 2
    scale = hd ** (-0.5)

    loads = [
        pltpu.make_async_copy(src, dst, in_sem.at[i])
        for i, (src, dst) in enumerate(
            [(tok_hbm, tok), (sq_hbm, sqraw), (init_hbm, init),
             (fg_hbm, fg), (sp_hbm, spraw), (wout_hbm, wo.at[:, head])]
        )
    ]
    pieces = [pl.ds(i * wraw.shape[0] // 4, wraw.shape[0] // 4) for i in range(4)]
    weights = [
        pltpu.make_async_copy(wqkv_hbm.at[piece], wraw.at[piece], w_sem.at[i])
        for i, piece in enumerate(pieces)
    ]
    for load in weights:
        load.start()
    for load in loads:
        load.start()

    barrier = pltpu.get_barrier_semaphore()
    peers = [head + 1 - 2 * lax.rem(head, 2), lax.rem(head + 2, 4), 3 - head]
    for peer in peers:
        pl.semaphore_signal(barrier, inc=1, device_id={"head": peer}, device_id_type=MESH)
    pl.semaphore_signal(barrier, inc=1, device_id={"book": core_mate}, device_id_type=MESH)
    pl.semaphore_signal(barrier, inc=1, device_id={"book": side_mate}, device_id_type=MESH)
    pl.semaphore_signal(barrier, inc=1, device_id={"seq": 1 - seq}, device_id_type=MESH)

    mine = pl.ds(pl.multiple_of(core * part_rows, part_rows), part_rows)

    def remote(src, dst, send, recv, goal):
        return pltpu.make_async_remote_copy(
            src_ref=src, dst_ref=dst, send_sem=send, recv_sem=recv,
            device_id=goal, device_id_type=MESH,
        )

    wz = [remote(wout_hbm.at[:, mine], wo.at[:, head, mine], wz_send.at[0], wz_recv.at[0],
                 {"head": peers[0]})]
    near = [wo.at[:, peers[0], mine]]
    for i in (1, 2):
        wz.append(remote(wout_hbm.at[side, mine], wo.at[side, head, mine], wz_send.at[i],
                         wz_recv.at[i], {"head": peers[i]}))
        near.append(wo.at[side, peers[i], mine])
    wc = [
        remote(near[i], near[i], wc_send.at[i], wc_recv.at[i], {"book": core_mate})
        for i in range(3)
    ]
    wy, wd = [], []
    for i in (1, 2):
        across = wo.at[1 - side, peers[i], mine]
        wy.append(remote(near[i], near[i], wy_send.at[i - 1], wy_recv.at[i - 1],
                         {"book": side_mate}))
        wd.append(remote(across, across, wd_send.at[i - 1], wd_recv.at[i - 1],
                         {"book": core_mate}))

    def kv_copy(idx, src, dst):
        return remote(src, dst, kv_send.at[idx], kv_recv.at[idx], {"seq": 1 - seq})

    kv = [kv_copy(0, fg_hbm, fg0)]
    for h in range(n_loc):
        kv.append(kv_copy(1 + 2 * h, kcat.at[h, pl.ds(W, W)], kcat.at[h, pl.ds(0, W)]))
        kv.append(kv_copy(2 + 2 * h, vcat.at[h, pl.ds(W, W)], vcat.at[h, pl.ds(0, W)]))

    pl.semaphore_wait(barrier, heads + 2)
    for copy in wz:
        copy.start()

    for load, piece in zip(weights, pieces):
        load.wait()
        wf[piece, :] = wraw[piece, :].astype(F32)
    period = 3 * n_loc

    def project(slot, columns):
        for i, column in enumerate(columns):
            w2[slot, :, i * hd:(i + 1) * hd] = wf[pl.ds(column, depth, stride=period), :].astype(BF16)
        return jnp.dot(tok[...], w2[slot], preferred_element_type=F32).astype(BF16)

    loads[0].wait()
    for h in range(n_loc):
        both = project(h, (n_loc + h, 2 * n_loc + h))
        kcat[h, W:, :] = both[:, :hd]
        vcat[h, W:, :] = both[:, hd:]

        @pl.when(seq == 0)
        def _():
            kv[1 + 2 * h].start()
            kv[2 + 2 * h].start()
            if h == 0:
                kv[0].start()

    queries = project(n_loc, range(n_loc))
    for h in range(n_loc):
        qb[h] = queries[:, h * hd:(h + 1) * hd]

    wz[0].wait_recv()
    wc[0].start()

    loads[1].wait()
    sqf[...] = sqraw[...].astype(F32)
    for h in range(n_loc):
        sqb[h] = sqf[pl.ds(h, slots, stride=n_loc), :].astype(BF16)
    loads[4].wait()
    spf[...] = spraw[...].astype(F32)
    loads[2].wait()
    loads[3].wait()

    tile = 256

    def slot_summary(h, row, off):
        scores = nt_dot(sqb[h, row:row + tile, :], kcat[h, off:off + W, :])
        top = jnp.max(scores, axis=1, keepdims=True)
        p = jnp.exp((scores - top) * scale)
        total = jnp.sum(p, axis=1, keepdims=True)
        part = jnp.dot(p.astype(BF16), vcat[h, off:off + W, :], preferred_element_type=F32)
        return part / total

    for h in range(n_loc):
        for row in range(0, slots, tile):
            summ[h, row:row + tile, :] = slot_summary(h, row, W)

    r_pos = lax.broadcasted_iota(jnp.int32, (rows, rows), 0)
    c_pos = lax.broadcasted_iota(jnp.int32, (rows, rows), 1)
    causal = c_pos <= r_pos

    def masked(scores, at, allowed):
        blocks = [scores[:, c:c + rows] for c in range(0, scores.shape[1], rows)]
        blocks[at] = jnp.where(allowed, blocks[at], -1e30)
        return jnp.concatenate(blocks, axis=1)

    for h in range(n_loc):
        for i in range(heads):
            q = qb[h, i * rows:(i + 1) * rows, :]
            stop = W + (i + 1) * rows
            scores = masked(nt_dot(q, kcat[h, W:stop, :]), i, causal)
            top = jnp.max(scores, axis=1, keepdims=True)
            p = jnp.exp((scores - top) * scale)
            own_max[h, i] = top
            own_sum[h, i] = jnp.sum(p, axis=1, keepdims=True)
            own_acc[h, i] = jnp.dot(p.astype(BF16), vcat[h, W:stop, :], preferred_element_type=F32)

    for i in (1, 2):
        wz[i].wait_recv()
        wy[i - 1].start()
        wc[i].start()

    def attend(h, i, with_prev):
        q = qb[h, i * rows:(i + 1) * rows, :]
        begin = i * rows
        far = nt_dot(q, skv[h, :, :hd])
        top = jnp.maximum(own_max[h, i], jnp.max(far, axis=1, keepdims=True))
        if with_prev:
            prev = masked(nt_dot(q, kcat[h, begin:W, :]), 0, jnp.logical_not(causal))
            top = jnp.maximum(top, jnp.max(prev, axis=1, keepdims=True))
        fade = jnp.exp((own_max[h, i] - top) * scale)
        p_far = jnp.exp((far - top) * scale)
        total = own_sum[h, i] * fade + jnp.sum(p_far, axis=1, keepdims=True)
        out = own_acc[h, i] * fade + jnp.dot(
            p_far.astype(BF16), skv[h, :, hd:], preferred_element_type=F32
        )
        if with_prev:
            p_prev = jnp.exp((prev - top) * scale)
            total = total + jnp.sum(p_prev, axis=1, keepdims=True)
            out = out + jnp.dot(
                p_prev.astype(BF16), vcat[h, begin:W, :], preferred_element_type=F32
            )
        att_out[h, i] = (out / total).astype(BF16)

    def at_copy(h, goal):
        return remote(att_out.at[h, goal], att.at[h, head], at_send.at[h, goal],
                      at_recv.at[h, head], {"head": goal})

    def at_arrival(h, origin):
        return remote(att_out.at[h, origin], att.at[h, origin], at_send.at[h, origin],
                      at_recv.at[h, origin], {"head": origin})

    for h in range(n_loc):
        @pl.when(seq == 0)
        def _():
            state[h] = init[pl.ds(h, slots, stride=n_loc), :]

        @pl.when(seq == 1)
        def _():
            if h == 0:
                kv[0].wait_recv()
            kv[1 + 2 * h].wait_recv()
            kv[2 + 2 * h].wait_recv()
            keep = fg0[h:h + 1, :]
            for row in range(0, slots, tile):
                first = init[pl.ds(h + n_loc * row, tile, stride=n_loc), :]
                state[h, row:row + tile, :] = keep * first + (1.0 - keep) * slot_summary(h, row, 0)

        base = h * 2 * hd
        proj = jnp.concatenate(
            [spf[pl.ds(base + c, hd, stride=2), :].astype(BF16) for c in range(2)], axis=1
        )
        skv[h] = jnp.dot(state[h].astype(BF16), proj, preferred_element_type=F32).astype(BF16)

        for group in ((0, 2), (1, 3)):
            for s in range(2):
                @pl.when(seq == s)
                def _():
                    for i in group:
                        attend(h, i, s == 1)

            for i in group:
                @pl.when(head != i)
                def _():
                    at_copy(h, i).start()

        keep = fg[h:h + 1, :]
        carried[pl.ds(h, slots, stride=n_loc), :] = keep * state[h] + (1.0 - keep) * summ[h]
        if h == 0:
            for i in range(2):
                wy[i].wait_recv()
                wd[i].start()

    carried_out = pltpu.make_async_copy(carried, carried_hbm, out_sem.at[0])
    carried_out.start()

    loads[5].wait()
    for copy in wc + wd:
        copy.wait_recv()
    for h in range(n_loc):
        att[h, head] = att_out[h, head]
        for peer in peers:
            at_arrival(h, peer).wait_recv()
        gathered = jnp.concatenate([att[h, o] for o in range(heads)], axis=1)
        share = jnp.dot(gathered, wo[h].reshape(heads * hd, depth), preferred_element_type=F32)
        acc = share if h == 0 else acc + share
    mixed[...] = acc.astype(BF16)
    mixed_out = pltpu.make_async_copy(mixed, mixed_hbm, out_sem.at[1])
    mixed_out.start()

    for copy in wz + wy + wc + wd:
        copy.wait_send()
    for h in range(n_loc):
        for peer in peers:
            at_copy(h, peer).wait_send()

    @pl.when(seq == 0)
    def _():
        for copy in kv:
            copy.wait_send()

    carried_out.wait()
    mixed_out.wait()


def fused_local(heads, tokens, w_qkv, w_out, slot_queries, state_proj, init_state, forget):
    tok_dev, depth = tokens.shape[1:]
    n_loc, hd = w_qkv.shape[2:]
    slots = slot_queries.shape[0]
    rows = tok_dev // heads
    period = 3 * n_loc
    anywhere = pl.BlockSpec(memory_space=pltpu.HBM)
    v = pltpu.VMEM
    dma = pltpu.SemaphoreType.DMA
    mixed, carried = pl.pallas_call(
        functools.partial(fused_kernel, heads),
        out_shape=(
            jax.ShapeDtypeStruct((rows, depth), BF16),
            jax.ShapeDtypeStruct((slots * n_loc, hd), F32),
        ),
        in_specs=[anywhere] * 7,
        out_specs=[pl.BlockSpec(memory_space=pl.ANY)] * 2,
        scratch_shapes=[
            v((tok_dev, depth), BF16),
            v((depth * period, hd), BF16),
            v((depth * period, hd), F32),
            v((3, depth, n_loc * hd), BF16),
            v((slots * n_loc, hd), BF16),
            v((slots * n_loc, hd), F32),
            v((n_loc, slots, hd), BF16),
            v((n_loc * hd * 2, hd), BF16),
            v((n_loc * hd * 2, hd), F32),
            v((slots * n_loc, hd), F32),
            v((n_loc, hd), F32),
            v((n_loc, hd), F32),
            v((n_loc, 2 * W, hd), BF16),
            v((n_loc, 2 * W, hd), BF16),
            v((n_loc, tok_dev, hd), BF16),
            v((n_loc, slots, hd), F32),
            v((n_loc, slots, hd), F32),
            v((n_loc, slots, 2 * hd), BF16),
            v((n_loc, heads, rows, hd), F32),
            v((n_loc, heads, rows, 1), F32),
            v((n_loc, heads, rows, 1), F32),
            v((slots * n_loc, hd), F32),
            v((n_loc, heads, hd, depth), BF16),
            v((n_loc, heads, rows, hd), BF16),
            v((n_loc, heads, rows, hd), BF16),
            v((rows, depth), BF16),
            dma((6,)),
            dma((4,)),
            dma((2,)),
            dma((1 + 2 * n_loc,)),
            dma((1 + 2 * n_loc,)),
            *[dma((heads - 1,)) for _ in range(8)],
            dma((n_loc, heads)),
            dma((n_loc, heads)),
        ],
        compiler_params=pltpu.CompilerParams(
            collective_id=0, has_side_effects=True, vmem_limit_bytes=48 * 1024 * 1024
        ),
        name="fused_layer",
    )(*[
        pltpu.with_memory_space_constraint(operand, pltpu.HBM)
        for operand in (
            tokens[0],
            w_qkv.reshape(depth * period, hd),
            w_out,
            slot_queries.reshape(slots * n_loc, hd),
            state_proj.reshape(n_loc * hd * 2, hd),
            init_state.reshape(slots * n_loc, hd),
            forget.reshape(n_loc, hd),
        )
    ])
    return mixed.reshape(1, rows, depth), carried.reshape(1, 1, slots, n_loc, hd)


def from_behind(block, axis, distance):
    devices = range(lax.axis_size(axis))
    route = [(i - distance, i) for i in devices if i - distance in devices]
    return lax.ppermute(block, axis, route)


def softmax_rows(scores):
    row_max = jnp.max(scores, axis=-1, keepdims=True)
    shifted = jnp.exp(scores - row_max)
    return shifted / jnp.sum(shifted, axis=-1, keepdims=True)


def local(tokens, w_qkv, w_out, slot_queries, state_proj, init_state, forget):
    tok_dev = tokens.shape[1]
    model_width = tokens.shape[2]
    head_count = w_qkv.shape[2]
    head_dim = w_qkv.shape[3]
    blocks_dev = tok_dev // W
    score_scale = head_dim ** (-0.5)
    projected = jnp.dot(
        tokens[0],
        w_qkv.reshape(model_width, 3 * head_count * head_dim),
        preferred_element_type=jnp.float32,
    )
    projected = projected.astype(jnp.bfloat16).reshape(tok_dev, 3, head_count, head_dim)
    query_rows = projected[:, 0]
    key_rows = projected[:, 1]
    value_rows = projected[:, 2]
    last_rows = jnp.stack([key_rows, value_rows], axis=0)
    before = from_behind(last_rows, "seq", 1)
    position = lax.axis_index("seq")
    retain = forget[0]
    slot_scores = (
        jnp.einsum("shd,khd->hsk", slot_queries, key_rows, preferred_element_type=jnp.float32)
        * score_scale
    )
    slot_weights = softmax_rows(slot_scores).astype(jnp.bfloat16)
    summaries = [
        jnp.einsum("hsk,khd->shd", slot_weights, value_rows, preferred_element_type=jnp.float32)
    ]
    decay_all = jnp.ones((head_count, head_dim), jnp.float32)
    offset = jnp.zeros(summaries[0].shape, jnp.float32)
    block_idx = 0
    decay_all = decay_all * retain[block_idx]
    offset = retain[block_idx] * offset + (1.0 - retain[block_idx]) * summaries[block_idx]
    initial = init_state[0]

    def relay_step(round_idx, current):
        passed = from_behind(decay_all * current + offset, "seq", 1)
        return jnp.where(position == 0, initial, passed)

    arriving_state = lax.fori_loop(0, lax.axis_size("seq") - 1, relay_step, initial)
    carry_state = arriving_state
    row_pos = jnp.arange(W, dtype=jnp.int32)[:, None]
    col_pos = jnp.arange(2 * W + slot_queries.shape[0], dtype=jnp.int32)[None, :]
    block_idx = 0
    prev_keys = before[0]
    prev_values = before[1]
    state_kv = jnp.einsum(
        "shd,hdce->sche",
        carry_state.astype(jnp.bfloat16),
        state_proj,
        preferred_element_type=jnp.float32,
    ).astype(jnp.bfloat16)
    key_all = jnp.concatenate([prev_keys, key_rows, state_kv[:, 0]], axis=0)
    value_all = jnp.concatenate([prev_values, value_rows, state_kv[:, 1]], axis=0)
    token_scores = (
        jnp.einsum("qhd,khd->hqk", query_rows, key_all, preferred_element_type=jnp.float32)
        * score_scale
    )
    global_block = position * blocks_dev + block_idx
    local_ok = (
        (col_pos - W <= row_pos) & (col_pos > row_pos) & ((col_pos >= W) | (global_block > 0))
    )
    allowed = jnp.where(col_pos < 2 * W, local_ok, True)
    token_scores = jnp.where(allowed[None], token_scores, -1e30)
    weights = softmax_rows(token_scores).astype(jnp.bfloat16)
    attended_blocks = jnp.einsum(
        "hqk,khd->qhd", weights, value_all, preferred_element_type=jnp.float32
    ).astype(jnp.bfloat16)
    carry_state = retain[block_idx] * carry_state + (1.0 - retain[block_idx]) * summaries[block_idx]
    carried_blocks = [carry_state]
    attended = attended_blocks.reshape(tok_dev, head_count * head_dim)
    w_flat = w_out.reshape(head_count * head_dim, model_width)
    row_share = tok_dev // lax.axis_size("head")
    partial_out = jnp.dot(attended, w_flat, preferred_element_type=jnp.float32)
    mixed_rows = lax.psum_scatter(partial_out, "head", scatter_dimension=0, tiled=True)
    mixed = mixed_rows.astype(jnp.bfloat16).reshape(1, row_share, model_width)
    carried = jnp.stack(carried_blocks, axis=0)[None]
    return (mixed, carried)


def solution(mesh):
    placed = (
        P("book", "seq", None),
        P(None, None, "head", None),
        P("head", None, None),
        P(None, "head", None),
        P("head", None, None, None),
        P("book", None, "head", None),
        P("book", "seq", "head", None),
    )
    sizes = (mesh.shape["seq"], mesh.shape["book"], mesh.shape["head"])
    body = functools.partial(fused_local, 4) if sizes == (2, 4, 4) else local
    return jax.shard_map(
        body,
        mesh=mesh,
        in_specs=placed,
        out_specs=(P("book", ("seq", "head"), None), P("book", "seq", None, "head", None)),
        check_vma=False,
    )
```

```python
import functools
import jax
import jax.numpy as jnp
from jax import lax
from jax.experimental import pallas as pl
from jax.experimental.pallas import tpu as pltpu
from jax.sharding import PartitionSpec as P

W = 512
MESH = pl.DeviceIdType.MESH
F32 = jnp.float32
BF16 = jnp.bfloat16


def nt_dot(a, b):
    return lax.dot_general(a, b, (((1,), (1,)), ((), ())), preferred_element_type=F32)


def fused_kernel(
    heads, tok_hbm, wqkv_hbm, wout_hbm, sq_hbm, sp_hbm, init_hbm, fg_hbm,
    mixed_hbm, carried_hbm,
    tok, wraw, wf, w2, sqraw, sqf, sqb, spraw, spf, init, fg, fg0,
    kcat, vcat, qb, summ, state, skv, own_acc, own_max, own_sum, carried, wo, att, att_out, mixed,
    in_sem, w_sem, out_sem, kv_send, kv_recv, wz_send, wz_recv, wy_send, wy_recv,
    wc_send, wc_recv, wd_send, wd_recv, at_send, at_recv,
):
    seq = lax.axis_index("seq")
    book = lax.axis_index("book")
    head = lax.axis_index("head")
    core = lax.rem(book, 2)
    side = book // 2
    core_mate = book + 1 - 2 * core
    side_mate = lax.rem(book + 2, 4)
    hd = kcat.shape[2]
    n_loc = kcat.shape[0]
    slots = sqb.shape[1]
    depth = tok.shape[1]
    rows = att.shape[2]
    part_rows = hd // 2
    scale = hd ** (-0.5)

    loads = [
        pltpu.make_async_copy(src, dst, in_sem.at[i])
        for i, (src, dst) in enumerate(
            [(tok_hbm, tok), (sq_hbm, sqraw), (init_hbm, init),
             (fg_hbm, fg), (sp_hbm, spraw), (wout_hbm, wo.at[:, head])]
        )
    ]
    pieces = [pl.ds(i * wraw.shape[0] // 4, wraw.shape[0] // 4) for i in range(4)]
    weights = [
        pltpu.make_async_copy(wqkv_hbm.at[piece], wraw.at[piece], w_sem.at[i])
        for i, piece in enumerate(pieces)
    ]
    for load in weights:
        load.start()
    for load in loads:
        load.start()

    barrier = pltpu.get_barrier_semaphore()
    peers = [head + 1 - 2 * lax.rem(head, 2), lax.rem(head + 2, 4), 3 - head]
    for peer in peers:
        pl.semaphore_signal(barrier, inc=1, device_id={"head": peer}, device_id_type=MESH)
    pl.semaphore_signal(barrier, inc=1, device_id={"book": core_mate}, device_id_type=MESH)
    pl.semaphore_signal(barrier, inc=1, device_id={"book": side_mate}, device_id_type=MESH)
    pl.semaphore_signal(barrier, inc=1, device_id={"seq": 1 - seq}, device_id_type=MESH)

    mine = pl.ds(pl.multiple_of(core * part_rows, part_rows), part_rows)

    def remote(src, dst, send, recv, goal):
        return pltpu.make_async_remote_copy(
            src_ref=src, dst_ref=dst, send_sem=send, recv_sem=recv,
            device_id=goal, device_id_type=MESH,
        )

    wz = [remote(wout_hbm.at[:, mine], wo.at[:, head, mine], wz_send.at[0], wz_recv.at[0],
                 {"head": peers[0]})]
    near = [wo.at[:, peers[0], mine]]
    for i in (1, 2):
        wz.append(remote(wout_hbm.at[side, mine], wo.at[side, head, mine], wz_send.at[i],
                         wz_recv.at[i], {"head": peers[i]}))
        near.append(wo.at[side, peers[i], mine])
    wc = [
        remote(near[i], near[i], wc_send.at[i], wc_recv.at[i], {"book": core_mate})
        for i in range(3)
    ]
    wy, wd = [], []
    for i in (1, 2):
        across = wo.at[1 - side, peers[i], mine]
        wy.append(remote(near[i], near[i], wy_send.at[i - 1], wy_recv.at[i - 1],
                         {"book": side_mate}))
        wd.append(remote(across, across, wd_send.at[i - 1], wd_recv.at[i - 1],
                         {"book": core_mate}))

    def kv_copy(idx, src, dst):
        return remote(src, dst, kv_send.at[idx], kv_recv.at[idx], {"seq": 1 - seq})

    kv = [kv_copy(0, fg_hbm, fg0)]
    for h in range(n_loc):
        kv.append(kv_copy(1 + 2 * h, kcat.at[h, pl.ds(W, W)], kcat.at[h, pl.ds(0, W)]))
        kv.append(kv_copy(2 + 2 * h, vcat.at[h, pl.ds(W, W)], vcat.at[h, pl.ds(0, W)]))

    pl.semaphore_wait(barrier, heads + 2)
    for copy in wz:
        copy.start()

    for load, piece in zip(weights, pieces):
        load.wait()
        wf[piece, :] = wraw[piece, :].astype(F32)
    period = 3 * n_loc

    def project(slot, columns):
        for i, column in enumerate(columns):
            w2[slot, :, i * hd:(i + 1) * hd] = wf[pl.ds(column, depth, stride=period), :].astype(BF16)
        return jnp.dot(tok[...], w2[slot], preferred_element_type=F32).astype(BF16)

    loads[0].wait()
    for h in range(n_loc):
        both = project(h, (n_loc + h, 2 * n_loc + h))
        kcat[h, W:, :] = both[:, :hd]
        vcat[h, W:, :] = both[:, hd:]

        @pl.when(seq == 0)
        def _():
            kv[1 + 2 * h].start()
            kv[2 + 2 * h].start()
            if h == 0:
                kv[0].start()

    queries = project(n_loc, range(n_loc))
    for h in range(n_loc):
        qb[h] = queries[:, h * hd:(h + 1) * hd]

    wz[0].wait_recv()
    wc[0].start()

    loads[1].wait()
    sqf[...] = sqraw[...].astype(F32)
    for h in range(n_loc):
        sqb[h] = sqf[pl.ds(h, slots, stride=n_loc), :].astype(BF16)
    loads[4].wait()
    spf[...] = spraw[...].astype(F32)
    loads[2].wait()
    loads[3].wait()

    tile = 256

    def slot_summary(h, row, off):
        scores = nt_dot(sqb[h, row:row + tile, :], kcat[h, off:off + W, :])
        top = jnp.max(scores, axis=1, keepdims=True)
        p = jnp.exp((scores - top) * scale)
        total = jnp.sum(p, axis=1, keepdims=True)
        part = jnp.dot(p.astype(BF16), vcat[h, off:off + W, :], preferred_element_type=F32)
        return part / total

    for h in range(n_loc):
        for row in range(0, slots, tile):
            summ[h, row:row + tile, :] = slot_summary(h, row, W)

    r_pos = lax.broadcasted_iota(jnp.int32, (rows, rows), 0)
    c_pos = lax.broadcasted_iota(jnp.int32, (rows, rows), 1)
    causal = c_pos <= r_pos

    def masked(scores, at, allowed):
        blocks = [scores[:, c:c + rows] for c in range(0, scores.shape[1], rows)]
        blocks[at] = jnp.where(allowed, blocks[at], -1e30)
        return jnp.concatenate(blocks, axis=1)

    for h in range(n_loc):
        for i in range(heads):
            q = qb[h, i * rows:(i + 1) * rows, :]
            stop = W + (i + 1) * rows
            scores = masked(nt_dot(q, kcat[h, W:stop, :]), i, causal)
            top = jnp.max(scores, axis=1, keepdims=True)
            p = jnp.exp((scores - top) * scale)
            own_max[h, i] = top
            own_sum[h, i] = jnp.sum(p, axis=1, keepdims=True)
            own_acc[h, i] = jnp.dot(p.astype(BF16), vcat[h, W:stop, :], preferred_element_type=F32)

    def attend(h, i, with_prev):
        q = qb[h, i * rows:(i + 1) * rows, :]
        begin = i * rows
        far = nt_dot(q, skv[h, :, :hd])
        top = jnp.maximum(own_max[h, i], jnp.max(far, axis=1, keepdims=True))
        if with_prev:
            prev = masked(nt_dot(q, kcat[h, begin:W, :]), 0, jnp.logical_not(causal))
            top = jnp.maximum(top, jnp.max(prev, axis=1, keepdims=True))
        fade = jnp.exp((own_max[h, i] - top) * scale)
        p_far = jnp.exp((far - top) * scale)
        total = own_sum[h, i] * fade + jnp.sum(p_far, axis=1, keepdims=True)
        out = own_acc[h, i] * fade + jnp.dot(
            p_far.astype(BF16), skv[h, :, hd:], preferred_element_type=F32
        )
        if with_prev:
            p_prev = jnp.exp((prev - top) * scale)
            total = total + jnp.sum(p_prev, axis=1, keepdims=True)
            out = out + jnp.dot(
                p_prev.astype(BF16), vcat[h, begin:W, :], preferred_element_type=F32
            )
        att_out[h, i] = (out / total).astype(BF16)

    def at_copy(h, goal):
        return remote(att_out.at[h, goal], att.at[h, head], at_send.at[h, goal],
                      at_recv.at[h, head], {"head": goal})

    def at_arrival(h, origin):
        return remote(att_out.at[h, origin], att.at[h, origin], at_send.at[h, origin],
                      at_recv.at[h, origin], {"head": origin})

    for h in range(n_loc):
        @pl.when(seq == 0)
        def _():
            state[h] = init[pl.ds(h, slots, stride=n_loc), :]

        @pl.when(seq == 1)
        def _():
            if h == 0:
                kv[0].wait_recv()
            kv[1 + 2 * h].wait_recv()
            kv[2 + 2 * h].wait_recv()
            keep = fg0[h:h + 1, :]
            for row in range(0, slots, tile):
                first = init[pl.ds(h + n_loc * row, tile, stride=n_loc), :]
                state[h, row:row + tile, :] = keep * first + (1.0 - keep) * slot_summary(h, row, 0)

        base = h * 2 * hd
        proj = jnp.concatenate(
            [spf[pl.ds(base + c, hd, stride=2), :].astype(BF16) for c in range(2)], axis=1
        )
        skv[h] = jnp.dot(state[h].astype(BF16), proj, preferred_element_type=F32).astype(BF16)

        if h == 0:
            for i in (1, 2):
                wz[i].wait_recv()
                wy[i - 1].start()
                wc[i].start()

        for group in ((0, 2), (1, 3)):
            for s in range(2):
                @pl.when(seq == s)
                def _():
                    for i in group:
                        attend(h, i, s == 1)

            for i in group:
                @pl.when(head != i)
                def _():
                    at_copy(h, i).start()

        keep = fg[h:h + 1, :]
        carried[pl.ds(h, slots, stride=n_loc), :] = keep * state[h] + (1.0 - keep) * summ[h]
        if h == n_loc - 1:
            for i in range(2):
                wy[i].wait_recv()
                wd[i].start()

    carried_out = pltpu.make_async_copy(carried, carried_hbm, out_sem.at[0])
    carried_out.start()

    loads[5].wait()
    for copy in wc + wd:
        copy.wait_recv()
    for h in range(n_loc):
        att[h, head] = att_out[h, head]
        for peer in peers:
            at_arrival(h, peer).wait_recv()
        gathered = jnp.concatenate([att[h, o] for o in range(heads)], axis=1)
        share = jnp.dot(gathered, wo[h].reshape(heads * hd, depth), preferred_element_type=F32)
        acc = share if h == 0 else acc + share
    mixed[...] = acc.astype(BF16)
    mixed_out = pltpu.make_async_copy(mixed, mixed_hbm, out_sem.at[1])
    mixed_out.start()

    for copy in wz + wy + wc + wd:
        copy.wait_send()
    for h in range(n_loc):
        for peer in peers:
            at_copy(h, peer).wait_send()

    @pl.when(seq == 0)
    def _():
        for copy in kv:
            copy.wait_send()

    carried_out.wait()
    mixed_out.wait()


def fused_local(heads, tokens, w_qkv, w_out, slot_queries, state_proj, init_state, forget):
    tok_dev, depth = tokens.shape[1:]
    n_loc, hd = w_qkv.shape[2:]
    slots = slot_queries.shape[0]
    rows = tok_dev // heads
    period = 3 * n_loc
    anywhere = pl.BlockSpec(memory_space=pltpu.HBM)
    v = pltpu.VMEM
    dma = pltpu.SemaphoreType.DMA
    mixed, carried = pl.pallas_call(
        functools.partial(fused_kernel, heads),
        out_shape=(
            jax.ShapeDtypeStruct((rows, depth), BF16),
            jax.ShapeDtypeStruct((slots * n_loc, hd), F32),
        ),
        in_specs=[anywhere] * 7,
        out_specs=[pl.BlockSpec(memory_space=pl.ANY)] * 2,
        scratch_shapes=[
            v((tok_dev, depth), BF16),
            v((depth * period, hd), BF16),
            v((depth * period, hd), F32),
            v((3, depth, n_loc * hd), BF16),
            v((slots * n_loc, hd), BF16),
            v((slots * n_loc, hd), F32),
            v((n_loc, slots, hd), BF16),
            v((n_loc * hd * 2, hd), BF16),
            v((n_loc * hd * 2, hd), F32),
            v((slots * n_loc, hd), F32),
            v((n_loc, hd), F32),
            v((n_loc, hd), F32),
            v((n_loc, 2 * W, hd), BF16),
            v((n_loc, 2 * W, hd), BF16),
            v((n_loc, tok_dev, hd), BF16),
            v((n_loc, slots, hd), F32),
            v((n_loc, slots, hd), F32),
            v((n_loc, slots, 2 * hd), BF16),
            v((n_loc, heads, rows, hd), F32),
            v((n_loc, heads, rows, 1), F32),
            v((n_loc, heads, rows, 1), F32),
            v((slots * n_loc, hd), F32),
            v((n_loc, heads, hd, depth), BF16),
            v((n_loc, heads, rows, hd), BF16),
            v((n_loc, heads, rows, hd), BF16),
            v((rows, depth), BF16),
            dma((6,)),
            dma((4,)),
            dma((2,)),
            dma((1 + 2 * n_loc,)),
            dma((1 + 2 * n_loc,)),
            *[dma((heads - 1,)) for _ in range(8)],
            dma((n_loc, heads)),
            dma((n_loc, heads)),
        ],
        compiler_params=pltpu.CompilerParams(
            collective_id=0, has_side_effects=True, vmem_limit_bytes=48 * 1024 * 1024
        ),
        name="fused_layer",
    )(*[
        pltpu.with_memory_space_constraint(operand, pltpu.HBM)
        for operand in (
            tokens[0],
            w_qkv.reshape(depth * period, hd),
            w_out,
            slot_queries.reshape(slots * n_loc, hd),
            state_proj.reshape(n_loc * hd * 2, hd),
            init_state.reshape(slots * n_loc, hd),
            forget.reshape(n_loc, hd),
        )
    ])
    return mixed.reshape(1, rows, depth), carried.reshape(1, 1, slots, n_loc, hd)


def from_behind(block, axis, distance):
    devices = range(lax.axis_size(axis))
    route = [(i - distance, i) for i in devices if i - distance in devices]
    return lax.ppermute(block, axis, route)


def softmax_rows(scores):
    row_max = jnp.max(scores, axis=-1, keepdims=True)
    shifted = jnp.exp(scores - row_max)
    return shifted / jnp.sum(shifted, axis=-1, keepdims=True)


def local(tokens, w_qkv, w_out, slot_queries, state_proj, init_state, forget):
    tok_dev = tokens.shape[1]
    model_width = tokens.shape[2]
    head_count = w_qkv.shape[2]
    head_dim = w_qkv.shape[3]
    blocks_dev = tok_dev // W
    score_scale = head_dim ** (-0.5)
    projected = jnp.dot(
        tokens[0],
        w_qkv.reshape(model_width, 3 * head_count * head_dim),
        preferred_element_type=jnp.float32,
    )
    projected = projected.astype(jnp.bfloat16).reshape(tok_dev, 3, head_count, head_dim)
    query_rows = projected[:, 0]
    key_rows = projected[:, 1]
    value_rows = projected[:, 2]
    last_rows = jnp.stack([key_rows, value_rows], axis=0)
    before = from_behind(last_rows, "seq", 1)
    position = lax.axis_index("seq")
    retain = forget[0]
    slot_scores = (
        jnp.einsum("shd,khd->hsk", slot_queries, key_rows, preferred_element_type=jnp.float32)
        * score_scale
    )
    slot_weights = softmax_rows(slot_scores).astype(jnp.bfloat16)
    summaries = [
        jnp.einsum("hsk,khd->shd", slot_weights, value_rows, preferred_element_type=jnp.float32)
    ]
    decay_all = jnp.ones((head_count, head_dim), jnp.float32)
    offset = jnp.zeros(summaries[0].shape, jnp.float32)
    block_idx = 0
    decay_all = decay_all * retain[block_idx]
    offset = retain[block_idx] * offset + (1.0 - retain[block_idx]) * summaries[block_idx]
    initial = init_state[0]

    def relay_step(round_idx, current):
        passed = from_behind(decay_all * current + offset, "seq", 1)
        return jnp.where(position == 0, initial, passed)

    arriving_state = lax.fori_loop(0, lax.axis_size("seq") - 1, relay_step, initial)
    carry_state = arriving_state
    row_pos = jnp.arange(W, dtype=jnp.int32)[:, None]
    col_pos = jnp.arange(2 * W + slot_queries.shape[0], dtype=jnp.int32)[None, :]
    block_idx = 0
    prev_keys = before[0]
    prev_values = before[1]
    state_kv = jnp.einsum(
        "shd,hdce->sche",
        carry_state.astype(jnp.bfloat16),
        state_proj,
        preferred_element_type=jnp.float32,
    ).astype(jnp.bfloat16)
    key_all = jnp.concatenate([prev_keys, key_rows, state_kv[:, 0]], axis=0)
    value_all = jnp.concatenate([prev_values, value_rows, state_kv[:, 1]], axis=0)
    token_scores = (
        jnp.einsum("qhd,khd->hqk", query_rows, key_all, preferred_element_type=jnp.float32)
        * score_scale
    )
    global_block = position * blocks_dev + block_idx
    local_ok = (
        (col_pos - W <= row_pos) & (col_pos > row_pos) & ((col_pos >= W) | (global_block > 0))
    )
    allowed = jnp.where(col_pos < 2 * W, local_ok, True)
    token_scores = jnp.where(allowed[None], token_scores, -1e30)
    weights = softmax_rows(token_scores).astype(jnp.bfloat16)
    attended_blocks = jnp.einsum(
        "hqk,khd->qhd", weights, value_all, preferred_element_type=jnp.float32
    ).astype(jnp.bfloat16)
    carry_state = retain[block_idx] * carry_state + (1.0 - retain[block_idx]) * summaries[block_idx]
    carried_blocks = [carry_state]
    attended = attended_blocks.reshape(tok_dev, head_count * head_dim)
    w_flat = w_out.reshape(head_count * head_dim, model_width)
    row_share = tok_dev // lax.axis_size("head")
    partial_out = jnp.dot(attended, w_flat, preferred_element_type=jnp.float32)
    mixed_rows = lax.psum_scatter(partial_out, "head", scatter_dimension=0, tiled=True)
    mixed = mixed_rows.astype(jnp.bfloat16).reshape(1, row_share, model_width)
    carried = jnp.stack(carried_blocks, axis=0)[None]
    return (mixed, carried)


def solution(mesh):
    placed = (
        P("book", "seq", None),
        P(None, None, "head", None),
        P("head", None, None),
        P(None, "head", None),
        P("head", None, None, None),
        P("book", None, "head", None),
        P("book", "seq", "head", None),
    )
    sizes = (mesh.shape["seq"], mesh.shape["book"], mesh.shape["head"])
    body = functools.partial(fused_local, 4) if sizes == (2, 4, 4) else local
    return jax.shard_map(
        body,
        mesh=mesh,
        in_specs=placed,
        out_specs=(P("book", ("seq", "head"), None), P("book", "seq", None, "head", None)),
        check_vma=False,
    )
```

```python
import functools
import jax
import jax.numpy as jnp
from jax import lax
from jax.experimental import pallas as pl
from jax.experimental.pallas import tpu as pltpu
from jax.sharding import PartitionSpec as P

W = 512
MESH = pl.DeviceIdType.MESH
F32 = jnp.float32
BF16 = jnp.bfloat16


def nt_dot(a, b):
    return lax.dot_general(a, b, (((1,), (1,)), ((), ())), preferred_element_type=F32)


def fused_kernel(
    heads, tok_hbm, wqkv_hbm, wout_hbm, sq_hbm, sp_hbm, init_hbm, fg_hbm,
    mixed_hbm, carried_hbm,
    tok, wraw, wf, w2, sqraw, sqf, sqb, spraw, spf, init, fg, fg0,
    kcat, vcat, qb, summ, state, skv, own_acc, own_max, own_sum, carried, wo, att, att_out, mixed,
    in_sem, w_sem, out_sem, kv_send, kv_recv, wz_send, wz_recv, wy_send, wy_recv,
    wc_send, wc_recv, wd_send, wd_recv, at_send, at_recv,
):
    seq = lax.axis_index("seq")
    book = lax.axis_index("book")
    head = lax.axis_index("head")
    core = lax.rem(book, 2)
    side = book // 2
    core_mate = book + 1 - 2 * core
    side_mate = lax.rem(book + 2, 4)
    hd = kcat.shape[2]
    n_loc = kcat.shape[0]
    slots = sqb.shape[1]
    depth = tok.shape[1]
    rows = att.shape[2]
    part_rows = hd // 2
    scale = hd ** (-0.5)

    loads = [
        pltpu.make_async_copy(src, dst, in_sem.at[i])
        for i, (src, dst) in enumerate(
            [(tok_hbm, tok), (sq_hbm, sqraw), (init_hbm, init),
             (fg_hbm, fg), (sp_hbm, spraw), (wout_hbm, wo.at[:, head])]
        )
    ]
    pieces = [pl.ds(i * wraw.shape[0] // 4, wraw.shape[0] // 4) for i in range(4)]
    weights = [
        pltpu.make_async_copy(wqkv_hbm.at[piece], wraw.at[piece], w_sem.at[i])
        for i, piece in enumerate(pieces)
    ]
    for load in weights:
        load.start()
    for load in loads:
        load.start()

    barrier = pltpu.get_barrier_semaphore()
    peers = [head + 1 - 2 * lax.rem(head, 2), lax.rem(head + 2, 4), 3 - head]
    for peer in peers:
        pl.semaphore_signal(barrier, inc=1, device_id={"head": peer}, device_id_type=MESH)
    pl.semaphore_signal(barrier, inc=1, device_id={"book": core_mate}, device_id_type=MESH)
    pl.semaphore_signal(barrier, inc=1, device_id={"book": side_mate}, device_id_type=MESH)
    pl.semaphore_signal(barrier, inc=1, device_id={"seq": 1 - seq}, device_id_type=MESH)

    mine = pl.ds(pl.multiple_of(core * part_rows, part_rows), part_rows)

    def remote(src, dst, send, recv, goal):
        return pltpu.make_async_remote_copy(
            src_ref=src, dst_ref=dst, send_sem=send, recv_sem=recv,
            device_id=goal, device_id_type=MESH,
        )

    wz = [remote(wout_hbm.at[:, mine], wo.at[:, head, mine], wz_send.at[0], wz_recv.at[0],
                 {"head": peers[0]})]
    near = [wo.at[:, peers[0], mine]]
    for i in (1, 2):
        wz.append(remote(wout_hbm.at[side, mine], wo.at[side, head, mine], wz_send.at[i],
                         wz_recv.at[i], {"head": peers[i]}))
        near.append(wo.at[side, peers[i], mine])
    wc = [
        remote(near[i], near[i], wc_send.at[i], wc_recv.at[i], {"book": core_mate})
        for i in range(3)
    ]
    wy, wd = [], []
    for i in (1, 2):
        across = wo.at[1 - side, peers[i], mine]
        wy.append(remote(near[i], near[i], wy_send.at[i - 1], wy_recv.at[i - 1],
                         {"book": side_mate}))
        wd.append(remote(across, across, wd_send.at[i - 1], wd_recv.at[i - 1],
                         {"book": core_mate}))

    def kv_copy(idx, src, dst):
        return remote(src, dst, kv_send.at[idx], kv_recv.at[idx], {"seq": 1 - seq})

    kv = [kv_copy(0, fg_hbm, fg0)]
    for h in range(n_loc):
        kv.append(kv_copy(1 + 2 * h, kcat.at[h, pl.ds(W, W)], kcat.at[h, pl.ds(0, W)]))
        kv.append(kv_copy(2 + 2 * h, vcat.at[h, pl.ds(W, W)], vcat.at[h, pl.ds(0, W)]))

    pl.semaphore_wait(barrier, heads + 2)
    for copy in wz:
        copy.start()

    for load, piece in zip(weights, pieces):
        load.wait()
        wf[piece, :] = wraw[piece, :].astype(F32)
    period = 3 * n_loc

    def project(slot, columns):
        for i, column in enumerate(columns):
            w2[slot, :, i * hd:(i + 1) * hd] = wf[pl.ds(column, depth, stride=period), :].astype(BF16)
        return jnp.dot(tok[...], w2[slot], preferred_element_type=F32).astype(BF16)

    loads[0].wait()
    for h in range(n_loc):
        both = project(h, (n_loc + h, 2 * n_loc + h))
        kcat[h, W:, :] = both[:, :hd]
        vcat[h, W:, :] = both[:, hd:]

        @pl.when(seq == 0)
        def _():
            kv[1 + 2 * h].start()
            kv[2 + 2 * h].start()
            if h == 0:
                kv[0].start()

    queries = project(n_loc, range(n_loc))
    for h in range(n_loc):
        qb[h] = queries[:, h * hd:(h + 1) * hd]

    wz[0].wait_recv()
    wc[0].start()

    loads[1].wait()
    sqf[...] = sqraw[...].astype(F32)
    for h in range(n_loc):
        sqb[h] = sqf[pl.ds(h, slots, stride=n_loc), :].astype(BF16)
    loads[4].wait()
    spf[...] = spraw[...].astype(F32)
    loads[2].wait()
    loads[3].wait()

    tile = 256

    def slot_summary(h, row, off):
        scores = nt_dot(sqb[h, row:row + tile, :], kcat[h, off:off + W, :])
        top = jnp.max(scores, axis=1, keepdims=True)
        p = jnp.exp((scores - top) * scale)
        total = jnp.sum(p, axis=1, keepdims=True)
        part = jnp.dot(p.astype(BF16), vcat[h, off:off + W, :], preferred_element_type=F32)
        return part / total

    for h in range(n_loc):
        for row in range(0, slots, tile):
            summ[h, row:row + tile, :] = slot_summary(h, row, W)

    r_pos = lax.broadcasted_iota(jnp.int32, (rows, rows), 0)
    c_pos = lax.broadcasted_iota(jnp.int32, (rows, rows), 1)
    causal = c_pos <= r_pos

    def masked(scores, at, allowed):
        blocks = [scores[:, c:c + rows] for c in range(0, scores.shape[1], rows)]
        blocks[at] = jnp.where(allowed, blocks[at], -1e30)
        return jnp.concatenate(blocks, axis=1)

    for h in range(n_loc):
        for i in range(heads):
            q = qb[h, i * rows:(i + 1) * rows, :]
            stop = W + (i + 1) * rows
            scores = masked(nt_dot(q, kcat[h, W:stop, :]), i, causal)
            top = jnp.max(scores, axis=1, keepdims=True)
            p = jnp.exp((scores - top) * scale)
            own_max[h, i] = top
            own_sum[h, i] = jnp.sum(p, axis=1, keepdims=True)
            own_acc[h, i] = jnp.dot(p.astype(BF16), vcat[h, W:stop, :], preferred_element_type=F32)

    def attend(h, i, with_prev):
        q = qb[h, i * rows:(i + 1) * rows, :]
        begin = i * rows
        far = nt_dot(q, skv[h, :, :hd])
        top = jnp.maximum(own_max[h, i], jnp.max(far, axis=1, keepdims=True))
        if with_prev:
            prev = masked(nt_dot(q, kcat[h, begin:W, :]), 0, jnp.logical_not(causal))
            top = jnp.maximum(top, jnp.max(prev, axis=1, keepdims=True))
        fade = jnp.exp((own_max[h, i] - top) * scale)
        p_far = jnp.exp((far - top) * scale)
        total = own_sum[h, i] * fade + jnp.sum(p_far, axis=1, keepdims=True)
        out = own_acc[h, i] * fade + jnp.dot(
            p_far.astype(BF16), skv[h, :, hd:], preferred_element_type=F32
        )
        if with_prev:
            p_prev = jnp.exp((prev - top) * scale)
            total = total + jnp.sum(p_prev, axis=1, keepdims=True)
            out = out + jnp.dot(
                p_prev.astype(BF16), vcat[h, begin:W, :], preferred_element_type=F32
            )
        att_out[h, i] = (out / total).astype(BF16)

    def at_copy(h, goal):
        return remote(att_out.at[h, goal], att.at[h, head], at_send.at[h, goal],
                      at_recv.at[h, head], {"head": goal})

    def at_arrival(h, origin):
        return remote(att_out.at[h, origin], att.at[h, origin], at_send.at[h, origin],
                      at_recv.at[h, origin], {"head": origin})

    for h in range(n_loc):
        @pl.when(seq == 0)
        def _():
            state[h] = init[pl.ds(h, slots, stride=n_loc), :]

        @pl.when(seq == 1)
        def _():
            if h == 0:
                kv[0].wait_recv()
            kv[1 + 2 * h].wait_recv()
            kv[2 + 2 * h].wait_recv()
            keep = fg0[h:h + 1, :]
            for row in range(0, slots, tile):
                first = init[pl.ds(h + n_loc * row, tile, stride=n_loc), :]
                state[h, row:row + tile, :] = keep * first + (1.0 - keep) * slot_summary(h, row, 0)

        base = h * 2 * hd
        proj = jnp.concatenate(
            [spf[pl.ds(base + c, hd, stride=2), :].astype(BF16) for c in range(2)], axis=1
        )
        skv[h] = jnp.dot(state[h].astype(BF16), proj, preferred_element_type=F32).astype(BF16)

        for group in ((0, 2), (1, 3)):
            for s in range(2):
                @pl.when(seq == s)
                def _():
                    for i in group:
                        attend(h, i, s == 1)

            for i in group:
                @pl.when(head != i)
                def _():
                    at_copy(h, i).start()

        if h == 0:
            for i in (1, 2):
                wz[i].wait_recv()
                wy[i - 1].start()
                wc[i].start()

        keep = fg[h:h + 1, :]
        carried[pl.ds(h, slots, stride=n_loc), :] = keep * state[h] + (1.0 - keep) * summ[h]
        if h == n_loc - 1:
            for i in range(2):
                wy[i].wait_recv()
                wd[i].start()

    carried_out = pltpu.make_async_copy(carried, carried_hbm, out_sem.at[0])
    carried_out.start()

    loads[5].wait()
    for copy in wc + wd:
        copy.wait_recv()
    for h in range(n_loc):
        att[h, head] = att_out[h, head]
        for peer in peers:
            at_arrival(h, peer).wait_recv()
        gathered = jnp.concatenate([att[h, o] for o in range(heads)], axis=1)
        share = jnp.dot(gathered, wo[h].reshape(heads * hd, depth), preferred_element_type=F32)
        acc = share if h == 0 else acc + share
    mixed[...] = acc.astype(BF16)
    mixed_out = pltpu.make_async_copy(mixed, mixed_hbm, out_sem.at[1])
    mixed_out.start()

    for copy in wz + wy + wc + wd:
        copy.wait_send()
    for h in range(n_loc):
        for peer in peers:
            at_copy(h, peer).wait_send()

    @pl.when(seq == 0)
    def _():
        for copy in kv:
            copy.wait_send()

    carried_out.wait()
    mixed_out.wait()


def fused_local(heads, tokens, w_qkv, w_out, slot_queries, state_proj, init_state, forget):
    tok_dev, depth = tokens.shape[1:]
    n_loc, hd = w_qkv.shape[2:]
    slots = slot_queries.shape[0]
    rows = tok_dev // heads
    period = 3 * n_loc
    anywhere = pl.BlockSpec(memory_space=pltpu.HBM)
    v = pltpu.VMEM
    dma = pltpu.SemaphoreType.DMA
    mixed, carried = pl.pallas_call(
        functools.partial(fused_kernel, heads),
        out_shape=(
            jax.ShapeDtypeStruct((rows, depth), BF16),
            jax.ShapeDtypeStruct((slots * n_loc, hd), F32),
        ),
        in_specs=[anywhere] * 7,
        out_specs=[pl.BlockSpec(memory_space=pl.ANY)] * 2,
        scratch_shapes=[
            v((tok_dev, depth), BF16),
            v((depth * period, hd), BF16),
            v((depth * period, hd), F32),
            v((3, depth, n_loc * hd), BF16),
            v((slots * n_loc, hd), BF16),
            v((slots * n_loc, hd), F32),
            v((n_loc, slots, hd), BF16),
            v((n_loc * hd * 2, hd), BF16),
            v((n_loc * hd * 2, hd), F32),
            v((slots * n_loc, hd), F32),
            v((n_loc, hd), F32),
            v((n_loc, hd), F32),
            v((n_loc, 2 * W, hd), BF16),
            v((n_loc, 2 * W, hd), BF16),
            v((n_loc, tok_dev, hd), BF16),
            v((n_loc, slots, hd), F32),
            v((n_loc, slots, hd), F32),
            v((n_loc, slots, 2 * hd), BF16),
            v((n_loc, heads, rows, hd), F32),
            v((n_loc, heads, rows, 1), F32),
            v((n_loc, heads, rows, 1), F32),
            v((slots * n_loc, hd), F32),
            v((n_loc, heads, hd, depth), BF16),
            v((n_loc, heads, rows, hd), BF16),
            v((n_loc, heads, rows, hd), BF16),
            v((rows, depth), BF16),
            dma((6,)),
            dma((4,)),
            dma((2,)),
            dma((1 + 2 * n_loc,)),
            dma((1 + 2 * n_loc,)),
            *[dma((heads - 1,)) for _ in range(8)],
            dma((n_loc, heads)),
            dma((n_loc, heads)),
        ],
        compiler_params=pltpu.CompilerParams(
            collective_id=0, has_side_effects=True, vmem_limit_bytes=48 * 1024 * 1024
        ),
        name="fused_layer",
    )(*[
        pltpu.with_memory_space_constraint(operand, pltpu.HBM)
        for operand in (
            tokens[0],
            w_qkv.reshape(depth * period, hd),
            w_out,
            slot_queries.reshape(slots * n_loc, hd),
            state_proj.reshape(n_loc * hd * 2, hd),
            init_state.reshape(slots * n_loc, hd),
            forget.reshape(n_loc, hd),
        )
    ])
    return mixed.reshape(1, rows, depth), carried.reshape(1, 1, slots, n_loc, hd)


def from_behind(block, axis, distance):
    devices = range(lax.axis_size(axis))
    route = [(i - distance, i) for i in devices if i - distance in devices]
    return lax.ppermute(block, axis, route)


def softmax_rows(scores):
    row_max = jnp.max(scores, axis=-1, keepdims=True)
    shifted = jnp.exp(scores - row_max)
    return shifted / jnp.sum(shifted, axis=-1, keepdims=True)


def local(tokens, w_qkv, w_out, slot_queries, state_proj, init_state, forget):
    tok_dev = tokens.shape[1]
    model_width = tokens.shape[2]
    head_count = w_qkv.shape[2]
    head_dim = w_qkv.shape[3]
    blocks_dev = tok_dev // W
    score_scale = head_dim ** (-0.5)
    projected = jnp.dot(
        tokens[0],
        w_qkv.reshape(model_width, 3 * head_count * head_dim),
        preferred_element_type=jnp.float32,
    )
    projected = projected.astype(jnp.bfloat16).reshape(tok_dev, 3, head_count, head_dim)
    query_rows = projected[:, 0]
    key_rows = projected[:, 1]
    value_rows = projected[:, 2]
    last_rows = jnp.stack([key_rows, value_rows], axis=0)
    before = from_behind(last_rows, "seq", 1)
    position = lax.axis_index("seq")
    retain = forget[0]
    slot_scores = (
        jnp.einsum("shd,khd->hsk", slot_queries, key_rows, preferred_element_type=jnp.float32)
        * score_scale
    )
    slot_weights = softmax_rows(slot_scores).astype(jnp.bfloat16)
    summaries = [
        jnp.einsum("hsk,khd->shd", slot_weights, value_rows, preferred_element_type=jnp.float32)
    ]
    decay_all = jnp.ones((head_count, head_dim), jnp.float32)
    offset = jnp.zeros(summaries[0].shape, jnp.float32)
    block_idx = 0
    decay_all = decay_all * retain[block_idx]
    offset = retain[block_idx] * offset + (1.0 - retain[block_idx]) * summaries[block_idx]
    initial = init_state[0]

    def relay_step(round_idx, current):
        passed = from_behind(decay_all * current + offset, "seq", 1)
        return jnp.where(position == 0, initial, passed)

    arriving_state = lax.fori_loop(0, lax.axis_size("seq") - 1, relay_step, initial)
    carry_state = arriving_state
    row_pos = jnp.arange(W, dtype=jnp.int32)[:, None]
    col_pos = jnp.arange(2 * W + slot_queries.shape[0], dtype=jnp.int32)[None, :]
    block_idx = 0
    prev_keys = before[0]
    prev_values = before[1]
    state_kv = jnp.einsum(
        "shd,hdce->sche",
        carry_state.astype(jnp.bfloat16),
        state_proj,
        preferred_element_type=jnp.float32,
    ).astype(jnp.bfloat16)
    key_all = jnp.concatenate([prev_keys, key_rows, state_kv[:, 0]], axis=0)
    value_all = jnp.concatenate([prev_values, value_rows, state_kv[:, 1]], axis=0)
    token_scores = (
        jnp.einsum("qhd,khd->hqk", query_rows, key_all, preferred_element_type=jnp.float32)
        * score_scale
    )
    global_block = position * blocks_dev + block_idx
    local_ok = (
        (col_pos - W <= row_pos) & (col_pos > row_pos) & ((col_pos >= W) | (global_block > 0))
    )
    allowed = jnp.where(col_pos < 2 * W, local_ok, True)
    token_scores = jnp.where(allowed[None], token_scores, -1e30)
    weights = softmax_rows(token_scores).astype(jnp.bfloat16)
    attended_blocks = jnp.einsum(
        "hqk,khd->qhd", weights, value_all, preferred_element_type=jnp.float32
    ).astype(jnp.bfloat16)
    carry_state = retain[block_idx] * carry_state + (1.0 - retain[block_idx]) * summaries[block_idx]
    carried_blocks = [carry_state]
    attended = attended_blocks.reshape(tok_dev, head_count * head_dim)
    w_flat = w_out.reshape(head_count * head_dim, model_width)
    row_share = tok_dev // lax.axis_size("head")
    partial_out = jnp.dot(attended, w_flat, preferred_element_type=jnp.float32)
    mixed_rows = lax.psum_scatter(partial_out, "head", scatter_dimension=0, tiled=True)
    mixed = mixed_rows.astype(jnp.bfloat16).reshape(1, row_share, model_width)
    carried = jnp.stack(carried_blocks, axis=0)[None]
    return (mixed, carried)


def solution(mesh):
    placed = (
        P("book", "seq", None),
        P(None, None, "head", None),
        P("head", None, None),
        P(None, "head", None),
        P("head", None, None, None),
        P("book", None, "head", None),
        P("book", "seq", "head", None),
    )
    sizes = (mesh.shape["seq"], mesh.shape["book"], mesh.shape["head"])
    body = functools.partial(fused_local, 4) if sizes == (2, 4, 4) else local
    return jax.shard_map(
        body,
        mesh=mesh,
        in_specs=placed,
        out_specs=(P("book", ("seq", "head"), None), P("book", "seq", None, "head", None)),
        check_vma=False,
    )
```
